256 devices in a mesh: tm: 32 (over x, z), space: 8 (over y, core).
Axes of the slice: x: 4, y: 4, z: 8, core: 2. Of those that a mesh axis runs over, the one named last changes fastest.
Arguments:
- increment: float32 [128, 4, 64, 512], P('tm', None, 'space'), may hold values from -6 to 6
- trajectory: float32 [128, 4, 64, 512], P('tm', None, 'space'), may hold values from -6 to 6
- input_weight: float32 [32, 4, 3, 3], replicated, may hold values from -1 to 1
- bias: float32 [32], replicated, may hold values from -4 to 4
- output_weight: float32 [4, 32, 3, 3], replicated, may hold values from -0.375 to 0.375
- correlation: float32 [4, 128, 128], replicated, may hold values from -1 to 4, as said below
Outputs:
- corrected: float32 [128, 4, 64, 512], P('tm', None, 'space')
The draws below stay inside these ranges and needn't reach their ends.
Inputs may be any that keep to these rules, and one draw needn't show every extreme that they name: `correlation`: each field's matrix is symmetric positive definite.
All inputs are finite; a program needn't handle non-finite values.
Results may differ from the reference program's by a relative error of at most 0.0001.
Values sent between devices are 32-bit elements; how exact they have to be, the bound alone decides.
A program may use at most 64 MiB of HBM per device.

```python
import jax
import jax.numpy as jnp
from jax import lax

FIELDS = 4
CHANNELS = 32
STEPS = 2
NX = 512
TIME = 128
NY = 64


def draw_correlation(key, part):
    base_rows = jax.random.uniform(key, (FIELDS, TIME, TIME), jnp.float32, -1.7, 1.7)
    gram = jnp.einsum('fik,fjk->fij', base_rows, base_rows) / TIME
    return 0.5 * jnp.eye(TIME, dtype=jnp.float32)[None] + gram


def shard_levels(stream_key, dims, split, smallest, largest):
    def one(dim, shards_of):
        steps = jax.random.uniform(jax.random.fold_in(jax.random.fold_in(stream_key, 6), dim), (shards_of,), jnp.float32, smallest / len(split), largest / len(split))
        return jnp.repeat(jnp.exp(steps), dims[dim] // shards_of).reshape((-1,) + (1,) * (len(dims) - dim - 1))

    level = one(*split[0])
    for cut in split[1:]:
        level = level * one(*cut)
    return level


def centred(stream_key, dims, deviation, reach, split=(), kind=jnp.bfloat16):
    factor_of = shard_levels(stream_key, dims, split, -0.22, 0.18) if split else 1.0
    entries = jax.random.normal(stream_key, dims, jnp.float32) * deviation * factor_of
    return jnp.minimum(jnp.maximum(entries, -reach), reach).astype(kind)


def setup_inputs(seed: int = 0) -> dict:
    arg_keys = jax.random.split(jax.random.key(seed), 7)
    return {
        "increment": centred(arg_keys[0], (TIME, FIELDS, NY, NX), 1.0, 6.0, ((0, 32), (2, 8)), jnp.float32),
        "trajectory": centred(arg_keys[1], (TIME, FIELDS, NY, NX), 1.0, 6.0, ((0, 32), (2, 8)), jnp.float32),
        "input_weight": centred(arg_keys[2], (CHANNELS, FIELDS, 3, 3), (FIELDS * 9) ** -0.5, 1.0, (), jnp.float32),
        "bias": centred(arg_keys[3], (CHANNELS,), 1.0, 4.0, (), jnp.float32),
        "output_weight": centred(arg_keys[4], (FIELDS, CHANNELS, 3, 3), (CHANNELS * 9) ** -0.5, 0.375, (), jnp.float32),
        "correlation": draw_correlation(jax.random.fold_in(arg_keys[6], 71), 0),
    }


tendency_scale = 0.5


def conv_same(field, weight):
    return lax.conv_general_dilated(field, weight, (1, 1), ((1, 1), (1, 1)), dimension_numbers=("NCHW", "OIHW", "NCHW"), precision=lax.Precision.HIGHEST)


def advance_time_slot(input_fields, input_weight, bias, output_weight):
    paired = jnp.stack([input_fields[0], input_fields[1]])
    for step_index in range(STEPS):
        mixed = conv_same(paired, input_weight)
        hidden = jnp.tanh(mixed[0] + bias[:, None, None])
        slope = (1.0 - hidden * hidden) * mixed[1]
        paired = paired + tendency_scale * conv_same(jnp.stack([hidden, slope]), output_weight)
    return paired[1]


def reference(increment, trajectory, input_weight, bias, output_weight, correlation):
    predicted_state = lax.map(lambda input_fields: advance_time_slot(input_fields, input_weight, bias, output_weight), (trajectory, increment))
    prior_state = jnp.concatenate([jnp.zeros_like(predicted_state[:1]), predicted_state[:-1]], axis=0)
    residual = increment - prior_state
    return jnp.einsum("fts,sfyx->tfyx", correlation, residual, precision=lax.Precision.HIGHEST)
```

```python
import functools

import jax
import jax.numpy as jnp
import numpy as np
from jax import lax
from jax.experimental import pallas as pl
from jax.experimental.pallas import tpu as pltpu
from jax.sharding import PartitionSpec as P

MESH = pl.DeviceIdType.MESH
F32, BF16 = jnp.float32, jnp.bfloat16
VMEM = pl.BlockSpec(memory_space=pltpu.VMEM)

ROWS, FIELDS, CHANNELS = 8, 4, 32
OWN = list(range(ROWS))
INNER = [-2, -1], [ROWS, ROWS + 1]
OUTER = [-4, -3], [ROWS + 2, ROWS + 3]
MID = list(range(-1, ROWS + 1)) + [-3, -2, ROWS + 1, ROWS + 2]
TAPS = 48


def block_rows(rows):
    return [(f, r) for f in range(FIELDS) for r in rows]


BLOCKS = [block_rows(OWN), block_rows(INNER[0]) + block_rows(INNER[1]), block_rows(OUTER[0]) + block_rows(OUTER[1])]


def columns_of(blocks):
    return [(b, f, r) for block in blocks for b in range(3) for f, r in block]


IN_COLS = columns_of(BLOCKS)
OUT_COLS = columns_of(BLOCKS[:2])


def selections():
    first = np.zeros((len(MID), TAPS, len(IN_COLS)), np.float32)
    second = np.zeros((4, len(OUT_COLS), 4 * TAPS), np.float32)
    for i, m in enumerate(MID):
        for k, (b, f, r) in enumerate(IN_COLS):
            a = r - m + 1
            if 0 <= a < 3:
                first[i, (a * 3 + b) * FIELDS + f, k] = 1.0
        for k, (b, f, r) in enumerate(OUT_COLS):
            a = m - r + 1
            if 0 <= a < 3:
                second[i // 4, k, i % 4 * TAPS + (a * 3 + b) * FIELDS + f] = 1.0
    return first, second


def split(x):
    high = x.astype(BF16)
    return high, (x - high.astype(F32)).astype(BF16)


def dot(a, b):
    return jnp.dot(a, b, preferred_element_type=F32)


def halo_kernel(
    inc, traj, w_in, w_bias, w_out, pick_in, pick_out, row_in, row_mid,
    top, bot, t1h, t1l, t2h, t2l, bias,
    down, up, taps_in, taps_out, send_sem, recv_sem,
):
    me = lax.axis_index("space")
    last = lax.axis_size("space") - 1
    barrier = pltpu.get_barrier_semaphore()

    @pl.when(me > 0)
    def _():
        pl.semaphore_signal(barrier, inc=1, device_id={"space": me - 1}, device_id_type=MESH)

    @pl.when(me < last)
    def _():
        pl.semaphore_signal(barrier, inc=1, device_id={"space": me + 1}, device_id_type=MESH)

    slots = inc.shape[0]
    for array, source in enumerate((traj, inc)):
        for j in range(slots):
            for f in range(FIELDS):
                down[array, j, 2 * f : 2 * f + 2, :] = source[j, f, 4:6, :]
                down[array, j, 8 + 2 * f : 10 + 2 * f, :] = source[j, f, 6:8, :]
                up[array, j, 2 * f : 2 * f + 2, :] = source[j, f, 0:2, :]
                up[array, j, 8 + 2 * f : 10 + 2 * f, :] = source[j, f, 2:4, :]

    pl.semaphore_wait(barrier, jnp.minimum(me, 1) + jnp.minimum(last - me, 1))

    def to_next():
        return pltpu.make_async_remote_copy(
            down, top, send_sem.at[0], recv_sem.at[0], device_id={"space": me + 1}, device_id_type=MESH
        )

    def to_previous():
        return pltpu.make_async_remote_copy(
            up, bot, send_sem.at[1], recv_sem.at[1], device_id={"space": me - 1}, device_id_type=MESH
        )

    @pl.when(me < last)
    def _():
        to_next().start()

    @pl.when(me > 0)
    def _():
        to_previous().start()

    grid_rows = (last + 1) * ROWS
    taps_in[...] = jnp.zeros_like(taps_in)
    taps_out[...] = jnp.zeros_like(taps_out)
    for a in range(3):
        for b in range(3):
            at = (a * 3 + b) * FIELDS
            taps_in[at : at + FIELDS, :CHANNELS] = w_in[a, b]
            w = 0.5 * w_out[a, b]
            for q in range(4):
                taps_out[q * TAPS + at : q * TAPS + at + FIELDS, q * CHANNELS : q * CHANNELS + CHANNELS] = w
    taps_in[36:37, :CHANNELS] = w_bias[...]
    w1 = jnp.transpose(taps_in[...])[:CHANNELS]
    bias[...] = jnp.broadcast_to(w1[:, 36:37], (CHANNELS, 128))
    w1s = jnp.concatenate(split(w1[:, :TAPS]), axis=0)
    row = row_in[...] + me * ROWS
    inside = jnp.where((row >= 0) & (row < grid_rows), 1.0, 0.0).astype(F32)
    for i in range(len(MID)):
        x = dot(w1s, pick_in[i]) * inside[0:1, :]
        t1h[32 * i : 32 * i + 32, :] = x[:CHANNELS].astype(BF16)
        t1l[32 * i : 32 * i + 32, :] = x[CHANNELS:].astype(BF16)
    w2h, w2l = split(taps_out[...])
    row = row_mid[...] + me * ROWS
    inside = jnp.where((row >= 0) & (row < grid_rows), 1.0, 0.0).astype(F32)
    for g in range(4):
        keep = inside[0:1, 128 * g : 128 * g + 128]
        t2h[:, 128 * g : 128 * g + 128] = (dot(pick_out[g], w2h) * keep).astype(BF16)
        t2l[:, 128 * g : 128 * g + 128] = (dot(pick_out[g], w2l) * keep).astype(BF16)

    @pl.when(me == 0)
    def _():
        top[...] = jnp.zeros_like(top)

    @pl.when(me == last)
    def _():
        bot[...] = jnp.zeros_like(bot)

    @pl.when(me < last)
    def _():
        to_next().wait_send()

    @pl.when(me > 0)
    def _():
        to_next().wait_recv()

    @pl.when(me > 0)
    def _():
        to_previous().wait_send()

    @pl.when(me < last)
    def _():
        to_previous().wait_recv()


def main_kernel(
    inc, traj, top, bot, t1h, t1l, t2h, t2l, bias, corr, perm,
    out,
    xh, xl, hh, hl, fore, before, rows, cols, results, back, cmat,
    c_sem, nb_send, nb_recv, f_send, f_recv, b_send, b_recv,
):
    nx = inc.shape[3]
    slots = inc.shape[0]
    depth = lax.axis_size("tm")
    width = depth // FIELDS
    me = lax.axis_index("tm")
    my_field, my_row = lax.div(me, width), lax.rem(me, width)

    barrier = pltpu.get_barrier_semaphore()

    def peer_of(p):
        return lax.rem(my_field + lax.div(p, width), FIELDS) * width + lax.rem(my_row + lax.rem(p, width), width)

    @pl.loop(1, depth)
    def _(p):
        pl.semaphore_signal(barrier, inc=1, device_id={"tm": peer_of(p)}, device_id_type=MESH)

    c_copy = pltpu.make_async_copy(corr.at[my_field], cmat, c_sem)
    c_copy.start()

    column = lax.broadcasted_iota(jnp.int32, (1, nx), 1)
    first, final = column == 0, column == nx - 1

    def shifted(x):
        left = jnp.where(first, 0.0, pltpu.roll(x, 1, 1))
        right = jnp.where(final, 0.0, pltpu.roll(x, nx - 1, 1))
        return left, x, right

    def put(x, row, lane):
        for piece in shifted(x):
            high, low = split(piece)
            xh[row : row + x.shape[0], lane : lane + nx] = high
            xl[row : row + x.shape[0], lane : lane + nx] = low
            row += x.shape[0]

    def three(ah, al, bh, bl):
        return dot(ah, bh) + dot(al, bh) + dot(ah, bl)

    def step(state, mids, outs):
        depth_in = 3 * sum(x.shape[0] for x in state[0])
        for array in range(2):
            at = 0
            for x in state[array]:
                put(x, at, array * nx)
                at += 3 * x.shape[0]
        lines = mids * CHANNELS
        for n in range(0, nx, 256):
            s, t = slice(n, n + 256), slice(nx + n, nx + n + 256)
            zs = three(t1h[:lines, :depth_in], t1l[:lines, :depth_in], xh[:depth_in, s], xl[:depth_in, s])
            zt = three(t1h[:lines, :depth_in], t1l[:lines, :depth_in], xh[:depth_in, t], xl[:depth_in, t])
            b = jnp.concatenate([bias[...], bias[...]], axis=1)
            h = jnp.tanh(zs.reshape(mids, CHANNELS, 256) + b[None]).reshape(lines, 256)
            g = (1.0 - h * h) * zt
            hh[:lines, s], hl[:lines, s] = split(h)
            hh[:lines, t], hl[:lines, t] = split(g)
        new = []
        for array in range(2):
            lane = slice(array * nx, array * nx + nx)
            taps = three(t2h[:outs, :lines], t2l[:outs, :lines], hh[:lines, lane], hl[:lines, lane])
            at, blocks = 0, []
            for x in state[array]:
                n = x.shape[0]
                if at >= outs:
                    break
                left = jnp.where(first, 0.0, pltpu.roll(taps[at : at + n], 1, 1))
                right = jnp.where(final, 0.0, pltpu.roll(taps[at + 2 * n : at + 3 * n], nx - 1, 1))
                blocks.append(x + (left + taps[at + n : at + 2 * n] + right))
                at += 3 * n
            new.append(blocks)
        return new

    def start_rows(j):
        pltpu.make_async_copy(rows.at[j, me], cols.at[j, me], f_recv.at[j]).start()

        @pl.loop(1, depth)
        def _(p):
            peer = peer_of(p)
            pltpu.make_async_remote_copy(
                rows.at[j, peer], cols.at[j, me], f_send.at[j], f_recv.at[j], device_id={"tm": peer}, device_id_type=MESH
            ).start()

    def send_residual(j, value):
        for q in range(nx // 128):
            rows[j, :, q, :] = value[:, 128 * q : 128 * q + 128]
        start_rows(j)

    after = lax.rem(me + 1, depth)
    to_after = pltpu.make_async_remote_copy(fore, before, nb_send, nb_recv, device_id={"tm": after}, device_id_type=MESH)

    @pl.loop(0, slots)
    def _(i):
        slot = lax.rem(i + slots - 1, slots)
        state = []
        for array, source in enumerate((traj, inc)):
            t, b = top[array, slot], bot[array, slot]
            own = source[slot].reshape(FIELDS * ROWS, nx)
            state.append(
                [own, jnp.concatenate([t[8:], b[:8]], axis=0), jnp.concatenate([t[:8], b[8:]], axis=0)]
            )
        state = step(state, len(MID), len(OUT_COLS))
        state = step(state, ROWS + 2, 3 * FIELDS * ROWS)
        forecast = state[1][0]

        @pl.when(i == 0)
        def _():
            pl.semaphore_wait(barrier, depth - 1)
            fore[...] = forecast
            to_after.start()

        @pl.when(i > 0)
        def _():
            send_residual(slot + 1, inc[slot + 1].reshape(FIELDS * ROWS, nx) - forecast)

        @pl.when(i == slots - 2)
        def _():
            to_after.wait()
            earlier = jnp.where(me == 0, 0.0, before[...])
            send_residual(0, inc[0].reshape(FIELDS * ROWS, nx) - earlier)

    c_copy.wait()
    ch, cl = split(cmat[...])
    ch = dot(ch, perm[...]).astype(BF16)
    cl = dot(cl, perm[...]).astype(BF16)
    for j in range(slots):
        pltpu.make_async_copy(cols.at[j], cols.at[j], f_recv.at[j]).wait()
    for q in range(nx // 128):
        v = jnp.concatenate([cols[j, :, q, :] for j in range(slots)], axis=0)
        vh, vl = split(v)
        r = three(ch, cl, vh, vl)
        results[:, q, :] = r
    pltpu.make_async_copy(results.at[pl.ds(me * slots, slots)], back.at[pl.ds(me * slots, slots)], b_recv).start()

    @pl.loop(1, depth)
    def _(p):
        peer = peer_of(p)
        pltpu.make_async_remote_copy(
            results.at[pl.ds(peer * slots, slots)],
            back.at[pl.ds(me * slots, slots)],
            b_send,
            b_recv,
            device_id={"tm": peer},
            device_id_type=MESH,
        ).start()

    pltpu.make_async_copy(back, back, b_recv).wait()
    for j in range(slots):
        for f in range(FIELDS):
            for q in range(nx // 128):
                lines = back.reshape(depth * slots * (nx // 128), 128)
                out[j, f, :, 128 * q : 128 * q + 128] = lines[
                    pl.ds(f * width * slots * 4 + j * 4 + q, ROWS, stride=slots * 4), :
                ]
    pltpu.make_async_copy(results.at[pl.ds(0, (depth - 1) * slots)], results.at[pl.ds(0, (depth - 1) * slots)], b_send).wait()
    for j in range(slots):
        pltpu.make_async_copy(rows.at[j, pl.ds(0, depth - 1)], rows.at[j, pl.ds(0, depth - 1)], f_send.at[j]).wait()


def body(increment, trajectory, input_weight, bias, output_weight, correlation):
    slots, fields, rows, nx = increment.shape
    pick_in, pick_out = selections()
    row_in = np.tile(np.array([r for _, _, r in IN_COLS], np.int32), (8, 1))
    depth = lax.axis_size("tm")
    time = correlation.shape[1]
    perm = np.zeros((time, time), np.float32)
    for e in range(depth):
        for j in range(slots):
            perm[e * slots + j, j * depth + e] = 1.0
    lines_mid = np.array([m for m in MID for _ in range(CHANNELS)] + [-1000] * (512 - 32 * len(MID)), np.int32)
    row_mid = np.tile(lines_mid, (8, 1))
    mid, cin, cout = 32 * len(MID), len(IN_COLS), len(OUT_COLS)
    top, bot, t1h, t1l, t2h, t2l, bias_lines = pl.pallas_call(
        halo_kernel,
        out_shape=(
            jax.ShapeDtypeStruct((2, slots, 16, nx), F32),
            jax.ShapeDtypeStruct((2, slots, 16, nx), F32),
            jax.ShapeDtypeStruct((mid, cin), BF16),
            jax.ShapeDtypeStruct((mid, cin), BF16),
            jax.ShapeDtypeStruct((cout, 512), BF16),
            jax.ShapeDtypeStruct((cout, 512), BF16),
            jax.ShapeDtypeStruct((CHANNELS, 128), F32),
        ),
        in_specs=[VMEM] * 9,
        out_specs=(VMEM,) * 7,
        scratch_shapes=[
            pltpu.VMEM((2, slots, 16, nx), F32),
            pltpu.VMEM((2, slots, 16, nx), F32),
            pltpu.VMEM((128, 128), F32),
            pltpu.VMEM((4 * TAPS, 128), F32),
            pltpu.SemaphoreType.DMA((2,)),
            pltpu.SemaphoreType.DMA((2,)),
        ],
        compiler_params=pltpu.CompilerParams(collective_id=0, has_side_effects=True),
        name="halo",
    )(
        increment, trajectory,
        jnp.transpose(input_weight, (2, 3, 1, 0)), bias[None, :], jnp.transpose(output_weight, (2, 3, 0, 1)),
        jnp.asarray(pick_in, BF16), jnp.asarray(pick_out, BF16), jnp.asarray(row_in), jnp.asarray(row_mid),
    )
    return pl.pallas_call(
        main_kernel,
        out_shape=jax.ShapeDtypeStruct(increment.shape, F32),
        in_specs=[VMEM] * 9 + [pl.BlockSpec(memory_space=pl.ANY), VMEM],
        out_specs=VMEM,
        scratch_shapes=[
            pltpu.VMEM((cin, 2 * nx), BF16),
            pltpu.VMEM((cin, 2 * nx), BF16),
            pltpu.VMEM((mid, 2 * nx), BF16),
            pltpu.VMEM((mid, 2 * nx), BF16),
            pltpu.VMEM((fields * rows, nx), F32),
            pltpu.VMEM((fields * rows, nx), F32),
            pltpu.VMEM((slots, depth, nx // 128, 128), F32),
            pltpu.VMEM((slots, depth, nx // 128, 128), F32),
            pltpu.VMEM((time, nx // 128, 128), F32),
            pltpu.VMEM((time, nx // 128, 128), F32),
            pltpu.VMEM((time, time), F32),
            pltpu.SemaphoreType.DMA,
            pltpu.SemaphoreType.DMA,
            pltpu.SemaphoreType.DMA,
            pltpu.SemaphoreType.DMA((slots,)),
            pltpu.SemaphoreType.DMA((slots,)),
            pltpu.SemaphoreType.DMA,
            pltpu.SemaphoreType.DMA,
        ],
        compiler_params=pltpu.CompilerParams(collective_id=1, has_side_effects=True),
        name="cycle",
    )(increment, trajectory, top, bot, t1h, t1l, t2h, t2l, bias_lines, correlation, jnp.asarray(perm, BF16))


def solution(mesh):
    split_spec = P("tm", None, "space", None)
    return jax.shard_map(
        body,
        mesh=mesh,
        in_specs=(split_spec, split_spec, P(), P(), P(), P()),
        out_specs=split_spec,
        check_vma=False,
    )
```

```python
import functools

import jax
import jax.numpy as jnp
import numpy as np
from jax import lax
from jax.experimental import pallas as pl
from jax.experimental.pallas import tpu as pltpu
from jax.sharding import PartitionSpec as P

MESH = pl.DeviceIdType.MESH
F32, BF16 = jnp.float32, jnp.bfloat16
VMEM = pl.BlockSpec(memory_space=pltpu.VMEM)
HBM = pl.BlockSpec(memory_space=pl.ANY)

ROWS, FIELDS, CHANNELS = 8, 4, 32
PAIR = 2 * FIELDS
TAPS = 48
HALVES = ((-3, 3), (-1, 3))


def tap(a, b, f):
    return (a * 3 + b) * FIELDS + f


def selections():
    wide = np.zeros((4, 2 * TAPS, 9 * 3 * PAIR), np.float32)
    narrow = np.zeros((2, 2 * TAPS, 6 * 3 * PAIR), np.float32)
    for table, pairs in ((wide, 3), (narrow, 2)):
        third = pairs * 3 * PAIR
        for i in range(table.shape[0]):
            for k in range(pairs):
                for b in range(3):
                    for f in range(FIELDS):
                        for r in range(2):
                            a = 2 * k + r - i
                            if 0 <= a < 3:
                                line = (k * 3 + b) * PAIR + 2 * f + r
                                table[i, tap(a, b, f), line] = 1.0
                                table[i, tap(a, b, f), third + line] = 1.0
                                table[i, TAPS + tap(a, b, f), 2 * third + line] = 1.0
    out = np.zeros((2, 9 * PAIR, 4 * TAPS), np.float32)
    for k in range(3):
        for b in range(3):
            for f in range(FIELDS):
                for r in range(2):
                    for a in range(3):
                        i = 2 * k + r + a
                        out[i // 4, (k * 3 + b) * PAIR + 2 * f + r, i % 4 * TAPS + tap(a, b, f)] = 1.0
    return wide, narrow, out


def split(x):
    high = x.astype(BF16)
    return high, (x - high.astype(F32)).astype(BF16)


def dot(a, b):
    return jnp.dot(a, b, preferred_element_type=F32)


def three(ah, al, bh, bl):
    return dot(ah, bh) + dot(al, bh) + dot(ah, bl)


def cycle_kernel(
    inc_hbm, traj_hbm, w_in, w_bias, w_out, pick_wide, pick_narrow, pick_out, perm, corr,
    out,
    inc, traj, up, down, top, bot,
    taps_in, taps_out, bias, t1, t1n, t2h, t2l,
    xs, hh, hl, fore, before, rows, cols, results, back, cmat,
    in_sem, c_sem, halo_send, halo_recv, nb_send, nb_recv, f_send, f_recv, b_send, b_recv,
):
    slots, nx = inc.shape[0], inc.shape[3]
    quarter = nx // 128
    depth = lax.axis_size("tm")
    width = depth // FIELDS
    me = lax.axis_index("tm")
    my_field, my_row = lax.div(me, width), lax.rem(me, width)
    place = lax.axis_index("space")
    last = lax.axis_size("space") - 1
    order = [slots - 1] + list(range(slots - 1))

    barrier = pltpu.get_barrier_semaphore()

    def peer_of(p):
        return lax.rem(my_field + lax.div(p, width), FIELDS) * width + lax.rem(my_row + lax.rem(p, width), width)

    @pl.when(place > 0)
    def _():
        pl.semaphore_signal(barrier, inc=1, device_id={"space": place - 1}, device_id_type=MESH)

    @pl.when(place < last)
    def _():
        pl.semaphore_signal(barrier, inc=1, device_id={"space": place + 1}, device_id_type=MESH)

    def inputs(j):
        return (
            pltpu.make_async_copy(traj_hbm.at[j], traj.at[j], in_sem.at[0, j]),
            pltpu.make_async_copy(inc_hbm.at[j], inc.at[j], in_sem.at[1, j]),
        )

    for j in order:
        for copy in inputs(j):
            copy.start()

    @pl.loop(1, depth)
    def _(p):
        pl.semaphore_signal(barrier, inc=1, device_id={"tm": peer_of(p)}, device_id_type=MESH)

    c_copy = pltpu.make_async_copy(corr.at[my_field], cmat, c_sem)
    c_copy.start()

    def pack(j):
        for array, source in enumerate((traj, inc)):
            for f in range(FIELDS):
                for half, target in enumerate((up, down)):
                    for k in range(2):
                        r = 4 * half + 2 * k
                        target[j, array, PAIR * k + 2 * f : PAIR * k + 2 * f + 2, :] = source[j, f, r : r + 2, :]

    def to_next(j):
        return pltpu.make_async_remote_copy(
            down.at[j], top.at[j], halo_send.at[0, j], halo_recv.at[0, j],
            device_id={"space": place + 1}, device_id_type=MESH,
        )

    def to_previous(j):
        return pltpu.make_async_remote_copy(
            up.at[j], bot.at[j], halo_send.at[1, j], halo_recv.at[1, j],
            device_id={"space": place - 1}, device_id_type=MESH,
        )

    for n, j in enumerate(order):
        for copy in inputs(j):
            copy.wait()
        pack(j)
        if n == 0:
            pl.semaphore_wait(barrier, depth - 1 + jnp.minimum(place, 1) + jnp.minimum(last - place, 1))

        @pl.when(place < last)
        def _():
            to_next(j).start()

        @pl.when(place > 0)
        def _():
            to_previous(j).start()

    taps_in[...] = jnp.zeros_like(taps_in)
    taps_out[...] = jnp.zeros_like(taps_out)
    for a in range(3):
        for b in range(3):
            at = tap(a, b, 0)
            taps_in[at : at + FIELDS, :CHANNELS] = w_in[a, b]
            w = 0.5 * w_out[a, b]
            for q in range(4):
                taps_out[q * TAPS + at : q * TAPS + at + FIELDS, q * CHANNELS : q * CHANNELS + CHANNELS] = w
    taps_in[2 * TAPS : 2 * TAPS + 1, :CHANNELS] = w_bias[...]
    w = taps_in[:TAPS, :]
    high = w.astype(BF16).astype(F32)
    taps_in[:TAPS, :] = high
    taps_in[TAPS : 2 * TAPS, :] = w - high
    w = jnp.transpose(taps_in[...])[:CHANNELS]
    bias[...] = jnp.broadcast_to(w[:, 2 * TAPS : 2 * TAPS + 1], (CHANNELS, 128))
    w = w[:, : 2 * TAPS].astype(BF16)
    for i in range(4):
        t1[CHANNELS * i : CHANNELS * i + CHANNELS, :] = dot(w, pick_wide[i]).astype(BF16)
    for i in range(2):
        t1n[CHANNELS * i : CHANNELS * i + CHANNELS, :] = dot(w, pick_narrow[i]).astype(BF16)
    lane_row = lax.shift_right_logical(lax.broadcasted_iota(jnp.int32, (1, 128), 1), 5) + place * ROWS
    for part, target in zip(split(taps_out[...]), (t2h, t2l)):
        for g in range(2):
            x = dot(pick_out[g], part)
            for step_id in range(2):
                for half in range(2):
                    row = lane_row + (HALVES[step_id][half] + 4 * g)
                    keep = jnp.where((row >= 0) & (row < (last + 1) * ROWS), x, 0.0)
                    target[step_id, half, :, 128 * g : 128 * g + 128] = keep.astype(BF16)

    @pl.when(place == 0)
    def _():
        top[...] = jnp.zeros_like(top)

    @pl.when(place == last)
    def _():
        bot[...] = jnp.zeros_like(bot)

    column = lax.broadcasted_iota(jnp.int32, (1, nx), 1)
    first, final = column == 0, column == nx - 1

    def step(state, step_id):
        pairs = len(state[0])
        outs = pairs - 2
        mids = 2 * outs + 2
        highs, lows = [], []
        for k in range(pairs):
            high, low = [], []
            for array in range(2):
                x = state[array][k]
                left = jnp.where(first, 0.0, pltpu.roll(x, 1, 1))
                right = jnp.where(final, 0.0, pltpu.roll(x, nx - 1, 1))
                x = jnp.concatenate([left, x, right], axis=0)
                h = x.astype(BF16).astype(F32)
                high.append(h)
                low.append(x - h)
            highs.append(jnp.concatenate(high, axis=1))
            lows.append(jnp.concatenate(low, axis=1))
        at = 0
        spans = [(g, 3) for g in range(0, pairs - 2, 2)] + [(pairs - 2, 2)]
        for g, n in spans:
            high = highs[g : g + n]
            value = jnp.concatenate(high + lows[g : g + n] + high, axis=0).astype(BF16)
            xs[g // 2, : value.shape[0], :] = value
        b = jnp.concatenate([bias[...], bias[...]], axis=1)[None]
        for n in range(0, nx, 256):
            s, t = slice(n, n + 256), slice(nx + n, nx + n + 256)
            at = 0
            for g, count in spans:
                table, many = (t1, 4) if count == 3 else (t1n, 2)
                depth_in = 9 * count * PAIR
                zs = dot(table[...], xs[g // 2, :depth_in, s])
                zt = dot(table[...], xs[g // 2, :depth_in, t])
                h = jnp.tanh(zs.reshape(many, CHANNELS, 256) + b).reshape(many * CHANNELS, 256)
                slope = (1.0 - h * h) * zt
                lines = slice(at, at + many * CHANNELS)
                hh[lines, s], hl[lines, s] = split(h)
                hh[lines, t], hl[lines, t] = split(slope)
                at += many * CHANNELS
        new = [[], []]
        wide, deep = outs // 2, (outs + 2) * CHANNELS
        for array in range(2):
            lane = slice(array * nx, array * nx + nx)
            for half in range(2):
                start = half * outs * CHANNELS
                taps = three(
                    t2h[step_id, half, : 3 * PAIR * wide, :deep],
                    t2l[step_id, half, : 3 * PAIR * wide, :deep],
                    hh[start : start + deep, lane],
                    hl[start : start + deep, lane],
                )
                for k in range(wide):
                    left = jnp.where(first, 0.0, pltpu.roll(taps[3 * PAIR * k : 3 * PAIR * k + PAIR], 1, 1))
                    middle = taps[3 * PAIR * k + PAIR : 3 * PAIR * k + 2 * PAIR]
                    right = pltpu.roll(taps[3 * PAIR * k + 2 * PAIR : 3 * PAIR * k + 3 * PAIR], nx - 1, 1)
                    right = jnp.where(final, 0.0, right)
                    new[array].append(state[array][half * wide + k + 1] + (left + middle + right))
        return new

    def line_of(device):
        f, r = lax.div(device, width), lax.rem(device, width)
        return lax.div(r, 2) * PAIR + 2 * f + lax.rem(r, 2)

    def send_residual(j, value):
        for q in range(quarter):
            rows[j, :, q, :] = value[:, 128 * q : 128 * q + 128]
        pltpu.make_async_copy(rows.at[j, line_of(me)], cols.at[j, me], f_recv.at[j]).start()

        @pl.loop(1, depth)
        def _(p):
            peer = peer_of(p)
            pltpu.make_async_remote_copy(
                rows.at[j, line_of(peer)], cols.at[j, me], f_send.at[j], f_recv.at[j],
                device_id={"tm": peer}, device_id_type=MESH,
            ).start()

    def increment_lines(j):
        return jnp.concatenate([up[j, 1], down[j, 1]], axis=0)

    after = lax.rem(me + 1, depth)
    to_after = pltpu.make_async_remote_copy(fore, before, nb_send, nb_recv, device_id={"tm": after}, device_id_type=MESH)

    @pl.loop(0, slots)
    def _(i):
        slot = lax.rem(i + slots - 1, slots)

        @pl.when(place > 0)
        def _():
            to_next(slot).wait_recv()

        @pl.when(place < last)
        def _():
            to_previous(slot).wait_recv()

        state = []
        for array in range(2):
            parts = [x[slot, array] for x in (top, up, down, bot)]
            state.append([x[PAIR * k : PAIR * k + PAIR] for x in parts for k in range(2)])
        state = step(state, 0)
        for array in range(2):
            state[array][0] = jnp.where(place > 0, state[array][0], 0.0)
            state[array][-1] = jnp.where(place < last, state[array][-1], 0.0)
        state = step(state, 1)
        forecast = jnp.concatenate(state[1], axis=0)

        @pl.when(i == 0)
        def _():
            fore[...] = forecast
            to_after.start()

        @pl.when(i > 0)
        def _():
            send_residual(slot + 1, increment_lines(slot + 1) - forecast)

        @pl.when(i == slots - 2)
        def _():
            to_after.wait()
            earlier = jnp.where(me == 0, 0.0, before[...])
            send_residual(0, increment_lines(0) - earlier)

    c_copy.wait()
    ch, cl = split(cmat[...])
    ch = dot(ch, perm[...]).astype(BF16)
    cl = dot(cl, perm[...]).astype(BF16)
    for j in range(slots):
        pltpu.make_async_copy(cols.at[j], cols.at[j], f_recv.at[j]).wait()
    for q in range(quarter):
        v = jnp.concatenate([cols[j, :, q, :] for j in range(slots)], axis=0)
        results[:, q, :] = three(ch, cl, *split(v))
    mine = pl.ds(me * slots, slots)
    pltpu.make_async_copy(results.at[mine], back.at[mine], b_recv).start()

    @pl.loop(1, depth)
    def _(p):
        peer = peer_of(p)
        pltpu.make_async_remote_copy(
            results.at[pl.ds(peer * slots, slots)], back.at[mine], b_send, b_recv,
            device_id={"tm": peer}, device_id_type=MESH,
        ).start()

    pltpu.make_async_copy(back, back, b_recv).wait()
    lines = back.reshape(depth * slots * quarter, 128)
    for j in range(slots):
        for f in range(FIELDS):
            for q in range(quarter):
                out[j, f, :, 128 * q : 128 * q + 128] = lines[
                    pl.ds((f * width * slots + j) * quarter + q, ROWS, stride=slots * quarter), :
                ]
    rest = pl.ds(0, (depth - 1) * slots)
    pltpu.make_async_copy(results.at[rest], results.at[rest], b_send).wait()
    for j in range(slots):
        pltpu.make_async_copy(rows.at[j, pl.ds(0, depth - 1)], rows.at[j, pl.ds(0, depth - 1)], f_send.at[j]).wait()

        @pl.when(place < last)
        def _():
            to_next(j).wait_send()

        @pl.when(place > 0)
        def _():
            to_previous(j).wait_send()


def body(increment, trajectory, input_weight, bias, output_weight, correlation):
    slots, fields, rows, nx = increment.shape
    pick_wide, pick_narrow, pick_out = (jnp.asarray(x, BF16) for x in selections())
    depth = lax.axis_size("tm")
    time = correlation.shape[1]
    perm = np.zeros((time, time), np.float32)
    for e in range(depth):
        for j in range(slots):
            perm[e * slots + j, j * depth + e] = 1.0
    local = increment.shape
    halo = (slots, 2, 2 * PAIR, nx)
    hidden = (14 * CHANNELS, 2 * nx)
    message = (slots, depth, nx // 128, 128)
    dma = pltpu.SemaphoreType.DMA
    return pl.pallas_call(
        cycle_kernel,
        out_shape=jax.ShapeDtypeStruct(local, F32),
        in_specs=[HBM, HBM] + [VMEM] * 7 + [HBM],
        out_specs=VMEM,
        scratch_shapes=[
            pltpu.VMEM(local, F32),
            pltpu.VMEM(local, F32),
            pltpu.VMEM(halo, F32),
            pltpu.VMEM(halo, F32),
            pltpu.VMEM(halo, F32),
            pltpu.VMEM(halo, F32),
            pltpu.VMEM((128, 128), F32),
            pltpu.VMEM((4 * TAPS, 128), F32),
            pltpu.VMEM((CHANNELS, 128), F32),
            pltpu.VMEM((4 * CHANNELS, 27 * PAIR), BF16),
            pltpu.VMEM((2 * CHANNELS, 18 * PAIR), BF16),
            pltpu.VMEM((2, 2, 9 * PAIR, 256), BF16),
            pltpu.VMEM((2, 2, 9 * PAIR, 256), BF16),
            pltpu.VMEM((4, 27 * PAIR, 2 * nx), BF16),
            pltpu.VMEM(hidden, BF16),
            pltpu.VMEM(hidden, BF16),
            pltpu.VMEM((fields * rows, nx), F32),
            pltpu.VMEM((fields * rows, nx), F32),
            pltpu.VMEM(message, F32),
            pltpu.VMEM(message, F32),
            pltpu.VMEM((time, nx // 128, 128), F32),
            pltpu.VMEM((time, nx // 128, 128), F32),
            pltpu.VMEM((time, time), F32),
            dma((2, slots)), dma, dma((2, slots)), dma((2, slots)),
            dma, dma, dma((slots,)), dma((slots,)), dma, dma,
        ],
        compiler_params=pltpu.CompilerParams(collective_id=0, has_side_effects=True),
        name="cycle",
    )(
        increment, trajectory,
        jnp.transpose(input_weight, (2, 3, 1, 0)), bias[None, :], jnp.transpose(output_weight, (2, 3, 0, 1)),
        pick_wide, pick_narrow, pick_out, jnp.asarray(perm, BF16), correlation,
    )


def solution(mesh):
    split_spec = P("tm", None, "space", None)
    return jax.shard_map(
        body,
        mesh=mesh,
        in_specs=(split_spec, split_spec, P(), P(), P(), P()),
        out_specs=split_spec,
        check_vma=False,
    )
```

```python
import functools

import jax
import jax.numpy as jnp
import numpy as np
from jax import lax
from jax.experimental import pallas as pl
from jax.experimental.pallas import tpu as pltpu
from jax.sharding import PartitionSpec as P

MESH = pl.DeviceIdType.MESH
F32, BF16 = jnp.float32, jnp.bfloat16
VMEM = pl.BlockSpec(memory_space=pltpu.VMEM)
HBM = pl.BlockSpec(memory_space=pl.ANY)

ROWS, FIELDS, CHANNELS = 8, 4, 32
PAIR = 2 * FIELDS
TAPS = 48
HALVES = ((-3, 3), (-1, 3))


def tap(a, b, f):
    return (a * 3 + b) * FIELDS + f


def selections():
    wide = np.zeros((4, 2 * TAPS, 9 * 3 * PAIR), np.float32)
    narrow = np.zeros((2, 2 * TAPS, 6 * 3 * PAIR), np.float32)
    for table, pairs in ((wide, 3), (narrow, 2)):
        third = pairs * 3 * PAIR
        for i in range(table.shape[0]):
            for k in range(pairs):
                for b in range(3):
                    for f in range(FIELDS):
                        for r in range(2):
                            a = 2 * k + r - i
                            if 0 <= a < 3:
                                line = (k * 3 + b) * PAIR + 2 * f + r
                                table[i, tap(a, b, f), line] = 1.0
                                table[i, tap(a, b, f), third + line] = 1.0
                                table[i, TAPS + tap(a, b, f), 2 * third + line] = 1.0
    out = np.zeros((2, 9 * PAIR, 4 * TAPS), np.float32)
    for k in range(3):
        for b in range(3):
            for f in range(FIELDS):
                for r in range(2):
                    for a in range(3):
                        i = 2 * k + r + a
                        out[i // 4, (k * 3 + b) * PAIR + 2 * f + r, i % 4 * TAPS + tap(a, b, f)] = 1.0
    return wide, narrow, out


def far_first(wide, deep):
    offsets = [(p, q) for p in range(wide) for q in range(deep) if p or q]
    hops = lambda n, size: min(n, size - n)
    return sorted(offsets, key=lambda o: (-hops(o[0], wide) - hops(o[1], deep), -hops(o[1], deep), o))


def split(x):
    high = x.astype(BF16)
    return high, (x - high.astype(F32)).astype(BF16)


def dot(a, b):
    return jnp.dot(a, b, preferred_element_type=F32)


def three(ah, al, bh, bl):
    return dot(ah, bh) + dot(al, bh) + dot(ah, bl)


def cycle_kernel(
    inc_hbm, traj_hbm, w_in, w_bias, w_out, pick_wide, pick_narrow, pick_out, perm, corr,
    out,
    inc, traj, up, down, top, bot,
    taps_in, taps_out, bias, t1, t1n, t2h, t2l,
    xs, hh, hl, fore, before, rows, cols, results, back, cmat,
    in_sem, c_sem, halo_send, halo_recv, nb_send, nb_recv, f_send, f_recv, b_send, b_recv,
):
    slots, nx = inc.shape[0], inc.shape[3]
    quarter = nx // 128
    depth = lax.axis_size("tm")
    width = depth // FIELDS
    me = lax.axis_index("tm")
    my_field, my_row = lax.div(me, width), lax.rem(me, width)
    place = lax.axis_index("space")
    last = lax.axis_size("space") - 1
    order = [slots - 1] + list(range(slots - 1))

    barrier = pltpu.get_barrier_semaphore()

    fields = [my_field] + [lax.rem(my_field + p, FIELDS) for p in range(1, FIELDS)]
    strips = [my_row] + [lax.rem(my_row + p, width) for p in range(1, width)]
    peers = [(fields[p], strips[q]) for p, q in far_first(FIELDS, width)]

    def device(peer):
        return {"tm": peer[0] * width + peer[1]}

    @pl.when(place > 0)
    def _():
        pl.semaphore_signal(barrier, inc=1, device_id={"space": place - 1}, device_id_type=MESH)

    @pl.when(place < last)
    def _():
        pl.semaphore_signal(barrier, inc=1, device_id={"space": place + 1}, device_id_type=MESH)

    def inputs(j):
        return (
            pltpu.make_async_copy(traj_hbm.at[j], traj.at[j], in_sem.at[0, j]),
            pltpu.make_async_copy(inc_hbm.at[j], inc.at[j], in_sem.at[1, j]),
        )

    for j in order:
        for copy in inputs(j):
            copy.start()

    for peer in peers:
        pl.semaphore_signal(barrier, inc=1, device_id=device(peer), device_id_type=MESH)

    c_copy = pltpu.make_async_copy(corr.at[my_field], cmat, c_sem)
    c_copy.start()

    def pack(j):
        for array, source in enumerate((traj, inc)):
            for f in range(FIELDS):
                for half, target in enumerate((up, down)):
                    for k in range(2):
                        r = 4 * half + 2 * k
                        target[j, array, PAIR * k + 2 * f : PAIR * k + 2 * f + 2, :] = source[j, f, r : r + 2, :]

    def to_next(j):
        return pltpu.make_async_remote_copy(
            down.at[j], top.at[j], halo_send.at[0, j], halo_recv.at[0, j],
            device_id={"space": place + 1}, device_id_type=MESH,
        )

    def to_previous(j):
        return pltpu.make_async_remote_copy(
            up.at[j], bot.at[j], halo_send.at[1, j], halo_recv.at[1, j],
            device_id={"space": place - 1}, device_id_type=MESH,
        )

    for n, j in enumerate(order):
        for copy in inputs(j):
            copy.wait()
        pack(j)
        if n == 0:
            pl.semaphore_wait(barrier, depth - 1 + jnp.minimum(place, 1) + jnp.minimum(last - place, 1))

        @pl.when(place < last)
        def _():
            to_next(j).start()

        @pl.when(place > 0)
        def _():
            to_previous(j).start()

    taps_in[...] = jnp.zeros_like(taps_in)
    taps_out[...] = jnp.zeros_like(taps_out)
    for a in range(3):
        for b in range(3):
            at = tap(a, b, 0)
            taps_in[at : at + FIELDS, :CHANNELS] = w_in[a, b]
            w = 0.5 * w_out[a, b]
            for q in range(4):
                taps_out[q * TAPS + at : q * TAPS + at + FIELDS, q * CHANNELS : q * CHANNELS + CHANNELS] = w
    taps_in[2 * TAPS : 2 * TAPS + 1, :CHANNELS] = w_bias[...]
    w = taps_in[:TAPS, :]
    high = w.astype(BF16).astype(F32)
    taps_in[:TAPS, :] = high
    taps_in[TAPS : 2 * TAPS, :] = w - high
    w = jnp.transpose(taps_in[...])[:CHANNELS]
    bias[...] = jnp.broadcast_to(w[:, 2 * TAPS : 2 * TAPS + 1], (CHANNELS, 128))
    w = w[:, : 2 * TAPS].astype(BF16)
    for i in range(4):
        t1[CHANNELS * i : CHANNELS * i + CHANNELS, :] = dot(w, pick_wide[i]).astype(BF16)
    for i in range(2):
        t1n[CHANNELS * i : CHANNELS * i + CHANNELS, :] = dot(w, pick_narrow[i]).astype(BF16)
    lane_row = lax.shift_right_logical(lax.broadcasted_iota(jnp.int32, (1, 128), 1), 5) + place * ROWS
    for part, target in zip(split(taps_out[...]), (t2h, t2l)):
        for g in range(2):
            x = dot(pick_out[g], part)
            for step_id in range(2):
                for half in range(2):
                    row = lane_row + (HALVES[step_id][half] + 4 * g)
                    keep = jnp.where((row >= 0) & (row < (last + 1) * ROWS), x, 0.0)
                    target[step_id, half, :, 128 * g : 128 * g + 128] = keep.astype(BF16)

    @pl.when(place == 0)
    def _():
        top[...] = jnp.zeros_like(top)

    @pl.when(place == last)
    def _():
        bot[...] = jnp.zeros_like(bot)

    column = lax.broadcasted_iota(jnp.int32, (1, nx), 1)
    first, final = column == 0, column == nx - 1

    def step(state, step_id):
        pairs = len(state[0])
        outs = pairs - 2
        mids = 2 * outs + 2
        highs, lows = [], []
        for k in range(pairs):
            high, low = [], []
            for array in range(2):
                x = state[array][k]
                left = jnp.where(first, 0.0, pltpu.roll(x, 1, 1))
                right = jnp.where(final, 0.0, pltpu.roll(x, nx - 1, 1))
                x = jnp.concatenate([left, x, right], axis=0)
                h = x.astype(BF16).astype(F32)
                high.append(h)
                low.append(x - h)
            highs.append(jnp.concatenate(high, axis=1))
            lows.append(jnp.concatenate(low, axis=1))
        at = 0
        spans = [(g, 3) for g in range(0, pairs - 2, 2)] + [(pairs - 2, 2)]
        for g, n in spans:
            high = highs[g : g + n]
            value = jnp.concatenate(high + lows[g : g + n] + high, axis=0).astype(BF16)
            xs[g // 2, : value.shape[0], :] = value
        b = jnp.concatenate([bias[...], bias[...]], axis=1)[None]
        for n in range(0, nx, 256):
            s, t = slice(n, n + 256), slice(nx + n, nx + n + 256)
            at = 0
            for g, count in spans:
                table, many = (t1, 4) if count == 3 else (t1n, 2)
                depth_in = 9 * count * PAIR
                zs = dot(table[...], xs[g // 2, :depth_in, s])
                zt = dot(table[...], xs[g // 2, :depth_in, t])
                h = jnp.tanh(zs.reshape(many, CHANNELS, 256) + b).reshape(many * CHANNELS, 256)
                slope = (1.0 - h * h) * zt
                lines = slice(at, at + many * CHANNELS)
                hh[lines, s], hl[lines, s] = split(h)
                hh[lines, t], hl[lines, t] = split(slope)
                at += many * CHANNELS
        new = [[], []]
        wide, deep = outs // 2, (outs + 2) * CHANNELS
        for array in range(2):
            lane = slice(array * nx, array * nx + nx)
            for half in range(2):
                start = half * outs * CHANNELS
                taps = three(
                    t2h[step_id, half, : 3 * PAIR * wide, :deep],
                    t2l[step_id, half, : 3 * PAIR * wide, :deep],
                    hh[start : start + deep, lane],
                    hl[start : start + deep, lane],
                )
                for k in range(wide):
                    left = jnp.where(first, 0.0, pltpu.roll(taps[3 * PAIR * k : 3 * PAIR * k + PAIR], 1, 1))
                    middle = taps[3 * PAIR * k + PAIR : 3 * PAIR * k + 2 * PAIR]
                    right = pltpu.roll(taps[3 * PAIR * k + 2 * PAIR : 3 * PAIR * k + 3 * PAIR], nx - 1, 1)
                    right = jnp.where(final, 0.0, right)
                    new[array].append(state[array][half * wide + k + 1] + (left + middle + right))
        return new

    def line_of(peer):
        f, r = peer
        return lax.div(r, 2) * PAIR + 2 * f + lax.rem(r, 2)

    def send_residual(j, value):
        for q in range(quarter):
            rows[j, :, q, :] = value[:, 128 * q : 128 * q + 128]
        for peer in peers:
            pltpu.make_async_remote_copy(
                rows.at[j, line_of(peer)], cols.at[j, me], f_send.at[j], f_recv.at[j],
                device_id=device(peer), device_id_type=MESH,
            ).start()
        pltpu.make_async_copy(rows.at[j, line_of((my_field, my_row))], cols.at[j, me], f_recv.at[j]).start()

    def increment_lines(j):
        return jnp.concatenate([up[j, 1], down[j, 1]], axis=0)

    after = lax.rem(me + 1, depth)
    to_after = pltpu.make_async_remote_copy(fore, before, nb_send, nb_recv, device_id={"tm": after}, device_id_type=MESH)

    @pl.loop(0, slots)
    def _(i):
        slot = lax.rem(i + slots - 1, slots)

        @pl.when(place > 0)
        def _():
            to_next(slot).wait_recv()

        @pl.when(place < last)
        def _():
            to_previous(slot).wait_recv()

        state = []
        for array in range(2):
            parts = [x[slot, array] for x in (top, up, down, bot)]
            state.append([x[PAIR * k : PAIR * k + PAIR] for x in parts for k in range(2)])
        state = step(state, 0)
        for array in range(2):
            state[array][0] = jnp.where(place > 0, state[array][0], 0.0)
            state[array][-1] = jnp.where(place < last, state[array][-1], 0.0)
        state = step(state, 1)
        forecast = jnp.concatenate(state[1], axis=0)

        @pl.when(i == 0)
        def _():
            fore[...] = forecast
            to_after.start()

        @pl.when(i > 0)
        def _():
            send_residual(slot + 1, increment_lines(slot + 1) - forecast)

        @pl.when(i == slots - 2)
        def _():
            to_after.wait()
            earlier = jnp.where(me == 0, 0.0, before[...])
            send_residual(0, increment_lines(0) - earlier)

    c_copy.wait()
    ch, cl = split(cmat[...])
    ch = dot(ch, perm[...]).astype(BF16)
    cl = dot(cl, perm[...]).astype(BF16)
    for j in range(slots):
        pltpu.make_async_copy(cols.at[j], cols.at[j], f_recv.at[j]).wait()
    for q in range(quarter):
        v = jnp.concatenate([cols[j, :, q, :] for j in range(slots)], axis=0)
        results[:, q, :] = three(ch, cl, *split(v))
    mine = pl.ds(me * slots, slots)
    for peer in peers:
        pltpu.make_async_remote_copy(
            results.at[pl.ds((peer[0] * width + peer[1]) * slots, slots)], back.at[mine], b_send, b_recv,
            device_id=device(peer), device_id_type=MESH,
        ).start()
    pltpu.make_async_copy(results.at[mine], back.at[mine], b_recv).start()

    pltpu.make_async_copy(back, back, b_recv).wait()
    lines = back.reshape(depth * slots * quarter, 128)
    for j in range(slots):
        for f in range(FIELDS):
            for q in range(quarter):
                out[j, f, :, 128 * q : 128 * q + 128] = lines[
                    pl.ds((f * width * slots + j) * quarter + q, ROWS, stride=slots * quarter), :
                ]
    rest = pl.ds(0, (depth - 1) * slots)
    pltpu.make_async_copy(results.at[rest], results.at[rest], b_send).wait()
    for j in range(slots):
        pltpu.make_async_copy(rows.at[j, pl.ds(0, depth - 1)], rows.at[j, pl.ds(0, depth - 1)], f_send.at[j]).wait()

        @pl.when(place < last)
        def _():
            to_next(j).wait_send()

        @pl.when(place > 0)
        def _():
            to_previous(j).wait_send()


def body(increment, trajectory, input_weight, bias, output_weight, correlation):
    slots, fields, rows, nx = increment.shape
    pick_wide, pick_narrow, pick_out = (jnp.asarray(x, BF16) for x in selections())
    depth = lax.axis_size("tm")
    time = correlation.shape[1]
    perm = np.zeros((time, time), np.float32)
    for e in range(depth):
        for j in range(slots):
            perm[e * slots + j, j * depth + e] = 1.0
    local = increment.shape
    halo = (slots, 2, 2 * PAIR, nx)
    hidden = (14 * CHANNELS, 2 * nx)
    message = (slots, depth, nx // 128, 128)
    dma = pltpu.SemaphoreType.DMA
    return pl.pallas_call(
        cycle_kernel,
        out_shape=pltpu.VMEM(local, F32),
        in_specs=[HBM, HBM] + [VMEM] * 7 + [HBM],
        out_specs=VMEM,
        scratch_shapes=[
            pltpu.VMEM(local, F32),
            pltpu.VMEM(local, F32),
            pltpu.VMEM(halo, F32),
            pltpu.VMEM(halo, F32),
            pltpu.VMEM(halo, F32),
            pltpu.VMEM(halo, F32),
            pltpu.VMEM((128, 128), F32),
            pltpu.VMEM((4 * TAPS, 128), F32),
            pltpu.VMEM((CHANNELS, 128), F32),
            pltpu.VMEM((4 * CHANNELS, 27 * PAIR), BF16),
            pltpu.VMEM((2 * CHANNELS, 18 * PAIR), BF16),
            pltpu.VMEM((2, 2, 9 * PAIR, 256), BF16),
            pltpu.VMEM((2, 2, 9 * PAIR, 256), BF16),
            pltpu.VMEM((4, 27 * PAIR, 2 * nx), BF16),
            pltpu.VMEM(hidden, BF16),
            pltpu.VMEM(hidden, BF16),
            pltpu.VMEM((fields * rows, nx), F32),
            pltpu.VMEM((fields * rows, nx), F32),
            pltpu.VMEM(message, F32),
            pltpu.VMEM(message, F32),
            pltpu.VMEM((time, nx // 128, 128), F32),
            pltpu.VMEM((time, nx // 128, 128), F32),
            pltpu.VMEM((time, time), F32),
            dma((2, slots)), dma, dma((2, slots)), dma((2, slots)),
            dma, dma, dma((slots,)), dma((slots,)), dma, dma,
        ],
        compiler_params=pltpu.CompilerParams(collective_id=0, has_side_effects=True),
        name="cycle",
    )(
        increment, trajectory,
        jnp.transpose(input_weight, (2, 3, 1, 0)), bias[None, :], jnp.transpose(output_weight, (2, 3, 0, 1)),
        pick_wide, pick_narrow, pick_out, jnp.asarray(perm, BF16), correlation,
    )


def solution(mesh):
    split_spec = P("tm", None, "space", None)
    return jax.shard_map(
        body,
        mesh=mesh,
        in_specs=(split_spec, split_spec, P(), P(), P(), P()),
        out_specs=split_spec,
        check_vma=False,
    )
```

```python
import functools

import jax
import jax.numpy as jnp
import numpy as np
from jax import lax
from jax.experimental import pallas as pl
from jax.experimental.pallas import tpu as pltpu
from jax.sharding import PartitionSpec as P

MESH = pl.DeviceIdType.MESH
F32, BF16 = jnp.float32, jnp.bfloat16
VMEM = pl.BlockSpec(memory_space=pltpu.VMEM)
HBM = pl.BlockSpec(memory_space=pl.ANY)

ROWS, FIELDS, CHANNELS = 8, 4, 32
PAIR = 2 * FIELDS
TAPS = 48
HALVES = ((-3, 3), (-1, 3))


def tap(a, b, f):
    return (a * 3 + b) * FIELDS + f


def selections():
    wide = np.zeros((4, 2 * TAPS, 9 * 3 * PAIR), np.float32)
    narrow = np.zeros((2, 2 * TAPS, 6 * 3 * PAIR), np.float32)
    for table, pairs in ((wide, 3), (narrow, 2)):
        third = pairs * 3 * PAIR
        for i in range(table.shape[0]):
            for k in range(pairs):
                for b in range(3):
                    for f in range(FIELDS):
                        for r in range(2):
                            a = 2 * k + r - i
                            if 0 <= a < 3:
                                line = (k * 3 + b) * PAIR + 2 * f + r
                                table[i, tap(a, b, f), line] = 1.0
                                table[i, tap(a, b, f), third + line] = 1.0
                                table[i, TAPS + tap(a, b, f), 2 * third + line] = 1.0
    out = np.zeros((2, 9 * PAIR, 4 * TAPS), np.float32)
    for k in range(3):
        for b in range(3):
            for f in range(FIELDS):
                for r in range(2):
                    for a in range(3):
                        i = 2 * k + r + a
                        out[i // 4, (k * 3 + b) * PAIR + 2 * f + r, i % 4 * TAPS + tap(a, b, f)] = 1.0
    return wide, narrow, out


def far_first(wide, deep):
    offsets = [(p, q) for p in range(wide) for q in range(deep) if p or q]
    hops = lambda n, size: min(n, size - n)
    return sorted(offsets, key=lambda o: (-hops(o[0], wide) - hops(o[1], deep), -hops(o[1], deep), o))


def split(x):
    high = x.astype(BF16)
    return high, (x - high.astype(F32)).astype(BF16)


def dot(a, b):
    return jnp.dot(a, b, preferred_element_type=F32)


def three(ah, al, bh, bl):
    return dot(ah, bh) + dot(al, bh) + dot(ah, bl)


def cycle_kernel(
    inc_hbm, traj_hbm, *refs,
):
    count = 7
    tables_hbm, corr, refs = refs[:count], refs[count], refs[count + 1 :]
    out, tables, refs = refs[0], refs[1 : count + 1], refs[count + 1 :]
    cycle(inc_hbm, traj_hbm, tables_hbm, corr, out, tables, *refs)


def cycle(
    inc_hbm, traj_hbm, tables_hbm, corr, out, tables,
    inc, traj, up, down, top, bot,
    taps_in, taps_out, bias, t1, t1n, t2h, t2l,
    xs, hh, hl, fore, before, rows, cols, results, back, cmat,
    in_sem, table_sem, c_sem, met, halo_send, halo_recv, nb_send, nb_recv, f_send, f_recv, b_send, b_recv,
):
    slots, nx = inc.shape[0], inc.shape[3]
    quarter = nx // 128
    depth = lax.axis_size("tm")
    width = depth // FIELDS
    me = lax.axis_index("tm")
    my_field, my_row = lax.div(me, width), lax.rem(me, width)
    place = lax.axis_index("space")
    last = lax.axis_size("space") - 1
    order = [slots - 1] + list(range(slots - 1))

    barrier = pltpu.get_barrier_semaphore()

    fields = [my_field] + [lax.rem(my_field + p, FIELDS) for p in range(1, FIELDS)]
    strips = [my_row] + [lax.rem(my_row + p, width) for p in range(1, width)]
    peers = [(fields[p], strips[q]) for p, q in far_first(FIELDS, width)]

    def device(peer):
        return {"tm": peer[0] * width + peer[1]}

    beside = [(my_field, strips[1]), (my_field, strips[-1])]
    across = [(fields[1], my_row), (fields[-1], my_row)]

    def say(sem, devices):
        for d in devices:
            pl.semaphore_signal(sem, inc=1, device_id=device(d), device_id_type=MESH)

    w_in, w_bias, w_out, pick_wide, pick_narrow, pick_out, perm = tables

    @pl.when(place > 0)
    def _():
        pl.semaphore_signal(barrier, inc=1, device_id={"space": place - 1}, device_id_type=MESH)

    @pl.when(place < last)
    def _():
        pl.semaphore_signal(barrier, inc=1, device_id={"space": place + 1}, device_id_type=MESH)

    def inputs(j):
        return (
            pltpu.make_async_copy(traj_hbm.at[j], traj.at[j], in_sem.at[0, j]),
            pltpu.make_async_copy(inc_hbm.at[j], inc.at[j], in_sem.at[1, j]),
        )

    say(barrier, beside + across)
    for j in order:
        for copy in inputs(j):
            copy.start()

    table_copies = [pltpu.make_async_copy(*x, table_sem.at[n]) for n, x in enumerate(zip(tables_hbm, tables))]
    for copy in table_copies:
        copy.start()
    c_copy = pltpu.make_async_copy(corr.at[my_field], cmat, c_sem)
    c_copy.start()

    def pack(j):
        for array, source in enumerate((traj, inc)):
            for f in range(FIELDS):
                for half, target in enumerate((up, down)):
                    for k in range(2):
                        r = 4 * half + 2 * k
                        target[j, array, PAIR * k + 2 * f : PAIR * k + 2 * f + 2, :] = source[j, f, r : r + 2, :]

    def to_next(j):
        return pltpu.make_async_remote_copy(
            down.at[j], top.at[j], halo_send.at[0, j], halo_recv.at[0, j],
            device_id={"space": place + 1}, device_id_type=MESH,
        )

    def to_previous(j):
        return pltpu.make_async_remote_copy(
            up.at[j], bot.at[j], halo_send.at[1, j], halo_recv.at[1, j],
            device_id={"space": place - 1}, device_id_type=MESH,
        )

    for n, j in enumerate(order):
        for copy in inputs(j):
            copy.wait()
        pack(j)
        if n == 0:
            pl.semaphore_wait(barrier, 4 + jnp.minimum(place, 1) + jnp.minimum(last - place, 1))

        @pl.when(place < last)
        def _():
            to_next(j).start()

        @pl.when(place > 0)
        def _():
            to_previous(j).start()

    rounds = width // 2 - 1
    say(met.at[0], beside)
    for copy in table_copies:
        copy.wait()

    taps_in[...] = jnp.zeros_like(taps_in)
    taps_out[...] = jnp.zeros_like(taps_out)
    for a in range(3):
        for b in range(3):
            at = tap(a, b, 0)
            taps_in[at : at + FIELDS, :CHANNELS] = w_in[a, b]
            w = 0.5 * w_out[a, b]
            for q in range(4):
                taps_out[q * TAPS + at : q * TAPS + at + FIELDS, q * CHANNELS : q * CHANNELS + CHANNELS] = w
    taps_in[2 * TAPS : 2 * TAPS + 1, :CHANNELS] = w_bias[...]
    w = taps_in[:TAPS, :]
    high = w.astype(BF16).astype(F32)
    taps_in[:TAPS, :] = high
    taps_in[TAPS : 2 * TAPS, :] = w - high
    pl.semaphore_wait(met.at[0], 2)
    say(met.at[1], beside)
    w = jnp.transpose(taps_in[...])[:CHANNELS]
    bias[...] = jnp.broadcast_to(w[:, 2 * TAPS : 2 * TAPS + 1], (CHANNELS, 128))
    w = w[:, : 2 * TAPS].astype(BF16)
    for i in range(4):
        t1[CHANNELS * i : CHANNELS * i + CHANNELS, :] = dot(w, pick_wide[i]).astype(BF16)
    for i in range(2):
        t1n[CHANNELS * i : CHANNELS * i + CHANNELS, :] = dot(w, pick_narrow[i]).astype(BF16)
    for n in range(1, rounds):
        pl.semaphore_wait(met.at[n], 2)
        say(met.at[n + 1], beside if n + 1 < rounds else across)
    lane_row = lax.shift_right_logical(lax.broadcasted_iota(jnp.int32, (1, 128), 1), 5) + place * ROWS
    for part, target in zip(split(taps_out[...]), (t2h, t2l)):
        for g in range(2):
            x = dot(pick_out[g], part)
            for step_id in range(2):
                for half in range(2):
                    row = lane_row + (HALVES[step_id][half] + 4 * g)
                    keep = jnp.where((row >= 0) & (row < (last + 1) * ROWS), x, 0.0)
                    target[step_id, half, :, 128 * g : 128 * g + 128] = keep.astype(BF16)

    @pl.when(place == 0)
    def _():
        top[...] = jnp.zeros_like(top)

    @pl.when(place == last)
    def _():
        bot[...] = jnp.zeros_like(bot)

    column = lax.broadcasted_iota(jnp.int32, (1, nx), 1)
    first, final = column == 0, column == nx - 1

    def step(state, step_id):
        pairs = len(state[0])
        outs = pairs - 2
        mids = 2 * outs + 2
        highs, lows = [], []
        for k in range(pairs):
            high, low = [], []
            for array in range(2):
                x = state[array][k]
                left = jnp.where(first, 0.0, pltpu.roll(x, 1, 1))
                right = jnp.where(final, 0.0, pltpu.roll(x, nx - 1, 1))
                x = jnp.concatenate([left, x, right], axis=0)
                h = x.astype(BF16).astype(F32)
                high.append(h)
                low.append(x - h)
            highs.append(jnp.concatenate(high, axis=1))
            lows.append(jnp.concatenate(low, axis=1))
        at = 0
        spans = [(g, 3) for g in range(0, pairs - 2, 2)] + [(pairs - 2, 2)]
        for g, n in spans:
            high = highs[g : g + n]
            value = jnp.concatenate(high + lows[g : g + n] + high, axis=0).astype(BF16)
            xs[g // 2, : value.shape[0], :] = value
        b = jnp.concatenate([bias[...], bias[...]], axis=1)[None]
        for n in range(0, nx, 256):
            s, t = slice(n, n + 256), slice(nx + n, nx + n + 256)
            at = 0
            for g, count in spans:
                table, many = (t1, 4) if count == 3 else (t1n, 2)
                depth_in = 9 * count * PAIR
                zs = dot(table[...], xs[g // 2, :depth_in, s])
                zt = dot(table[...], xs[g // 2, :depth_in, t])
                h = jnp.tanh(zs.reshape(many, CHANNELS, 256) + b).reshape(many * CHANNELS, 256)
                slope = (1.0 - h * h) * zt
                lines = slice(at, at + many * CHANNELS)
                hh[lines, s], hl[lines, s] = split(h)
                hh[lines, t], hl[lines, t] = split(slope)
                at += many * CHANNELS
        new = [[], []]
        wide, deep = outs // 2, (outs + 2) * CHANNELS
        for array in range(2):
            lane = slice(array * nx, array * nx + nx)
            for half in range(2):
                start = half * outs * CHANNELS
                taps = three(
                    t2h[step_id, half, : 3 * PAIR * wide, :deep],
                    t2l[step_id, half, : 3 * PAIR * wide, :deep],
                    hh[start : start + deep, lane],
                    hl[start : start + deep, lane],
                )
                for k in range(wide):
                    left = jnp.where(first, 0.0, pltpu.roll(taps[3 * PAIR * k : 3 * PAIR * k + PAIR], 1, 1))
                    middle = taps[3 * PAIR * k + PAIR : 3 * PAIR * k + 2 * PAIR]
                    right = pltpu.roll(taps[3 * PAIR * k + 2 * PAIR : 3 * PAIR * k + 3 * PAIR], nx - 1, 1)
                    right = jnp.where(final, 0.0, right)
                    new[array].append(state[array][half * wide + k + 1] + (left + middle + right))
        return new

    def line_of(peer):
        f, r = peer
        return lax.div(r, 2) * PAIR + 2 * f + lax.rem(r, 2)

    def send_residual(j, value):
        for q in range(quarter):
            rows[j, :, q, :] = value[:, 128 * q : 128 * q + 128]
        for peer in peers:
            pltpu.make_async_remote_copy(
                rows.at[j, line_of(peer)], cols.at[j, me], f_send.at[j], f_recv.at[j],
                device_id=device(peer), device_id_type=MESH,
            ).start()
        pltpu.make_async_copy(rows.at[j, line_of((my_field, my_row))], cols.at[j, me], f_recv.at[j]).start()

    def increment_lines(j):
        return jnp.concatenate([up[j, 1], down[j, 1]], axis=0)

    after = lax.rem(me + 1, depth)
    to_after = pltpu.make_async_remote_copy(fore, before, nb_send, nb_recv, device_id={"tm": after}, device_id_type=MESH)

    @pl.loop(0, slots)
    def _(i):
        slot = lax.rem(i + slots - 1, slots)

        @pl.when(place > 0)
        def _():
            to_next(slot).wait_recv()

        @pl.when(place < last)
        def _():
            to_previous(slot).wait_recv()

        state = []
        for array in range(2):
            parts = [x[slot, array] for x in (top, up, down, bot)]
            state.append([x[PAIR * k : PAIR * k + PAIR] for x in parts for k in range(2)])
        state = step(state, 0)
        for array in range(2):
            state[array][0] = jnp.where(place > 0, state[array][0], 0.0)
            state[array][-1] = jnp.where(place < last, state[array][-1], 0.0)
        state = step(state, 1)
        forecast = jnp.concatenate(state[1], axis=0)

        @pl.when(i == 0)
        def _():
            fore[...] = forecast
            pl.semaphore_wait(met.at[rounds], 2)
            say(met.at[rounds + 1], across)
            to_after.start()

        @pl.when(i == 1)
        def _():
            pl.semaphore_wait(met.at[rounds + 1], 2)

        @pl.when(i > 0)
        def _():
            send_residual(slot + 1, increment_lines(slot + 1) - forecast)

        @pl.when(i == slots - 2)
        def _():
            to_after.wait()
            earlier = jnp.where(me == 0, 0.0, before[...])
            send_residual(0, increment_lines(0) - earlier)

    c_copy.wait()
    ch, cl = split(cmat[...])
    ch = dot(ch, perm[...]).astype(BF16)
    cl = dot(cl, perm[...]).astype(BF16)
    for j in range(slots):
        pltpu.make_async_copy(cols.at[j], cols.at[j], f_recv.at[j]).wait()
    for q in range(quarter):
        v = jnp.concatenate([cols[j, :, q, :] for j in range(slots)], axis=0)
        results[:, q, :] = three(ch, cl, *split(v))
    mine = pl.ds(me * slots, slots)
    for peer in peers:
        pltpu.make_async_remote_copy(
            results.at[pl.ds((peer[0] * width + peer[1]) * slots, slots)], back.at[mine], b_send, b_recv,
            device_id=device(peer), device_id_type=MESH,
        ).start()
    pltpu.make_async_copy(results.at[mine], back.at[mine], b_recv).start()

    pltpu.make_async_copy(back, back, b_recv).wait()
    lines = back.reshape(depth * slots * quarter, 128)
    for j in range(slots):
        for f in range(FIELDS):
            for q in range(quarter):
                out[j, f, :, 128 * q : 128 * q + 128] = lines[
                    pl.ds((f * width * slots + j) * quarter + q, ROWS, stride=slots * quarter), :
                ]
    rest = pl.ds(0, (depth - 1) * slots)
    pltpu.make_async_copy(results.at[rest], results.at[rest], b_send).wait()
    for j in range(slots):
        pltpu.make_async_copy(rows.at[j, pl.ds(0, depth - 1)], rows.at[j, pl.ds(0, depth - 1)], f_send.at[j]).wait()

        @pl.when(place < last)
        def _():
            to_next(j).wait_send()

        @pl.when(place > 0)
        def _():
            to_previous(j).wait_send()


def body(increment, trajectory, input_weight, bias, output_weight, correlation):
    slots, fields, rows, nx = increment.shape
    pick_wide, pick_narrow, pick_out = (jnp.asarray(x, BF16) for x in selections())
    depth = lax.axis_size("tm")
    time = correlation.shape[1]
    perm = np.zeros((time, time), np.float32)
    for e in range(depth):
        for j in range(slots):
            perm[e * slots + j, j * depth + e] = 1.0
    tables = (
        jnp.transpose(input_weight, (2, 3, 1, 0)), bias[None, :], jnp.transpose(output_weight, (2, 3, 0, 1)),
        pick_wide, pick_narrow, pick_out, jnp.asarray(perm, BF16),
    )
    local = increment.shape
    halo = (slots, 2, 2 * PAIR, nx)
    hidden = (14 * CHANNELS, 2 * nx)
    message = (slots, depth, nx // 128, 128)
    dma = pltpu.SemaphoreType.DMA
    return pl.pallas_call(
        cycle_kernel,
        out_shape=pltpu.VMEM(local, F32),
        in_specs=[HBM] * 10,
        out_specs=VMEM,
        scratch_shapes=[pltpu.VMEM(x.shape, x.dtype) for x in tables]
        + [
            pltpu.VMEM(local, F32),
            pltpu.VMEM(local, F32),
            pltpu.VMEM(halo, F32),
            pltpu.VMEM(halo, F32),
            pltpu.VMEM(halo, F32),
            pltpu.VMEM(halo, F32),
            pltpu.VMEM((128, 128), F32),
            pltpu.VMEM((4 * TAPS, 128), F32),
            pltpu.VMEM((CHANNELS, 128), F32),
            pltpu.VMEM((4 * CHANNELS, 27 * PAIR), BF16),
            pltpu.VMEM((2 * CHANNELS, 18 * PAIR), BF16),
            pltpu.VMEM((2, 2, 9 * PAIR, 256), BF16),
            pltpu.VMEM((2, 2, 9 * PAIR, 256), BF16),
            pltpu.VMEM((4, 27 * PAIR, 2 * nx), BF16),
            pltpu.VMEM(hidden, BF16),
            pltpu.VMEM(hidden, BF16),
            pltpu.VMEM((fields * rows, nx), F32),
            pltpu.VMEM((fields * rows, nx), F32),
            pltpu.VMEM(message, F32),
            pltpu.VMEM(message, F32),
            pltpu.VMEM((time, nx // 128, 128), F32),
            pltpu.VMEM((time, nx // 128, 128), F32),
            pltpu.VMEM((time, time), F32),
            dma((2, slots)), dma((len(tables),)), dma, pltpu.SemaphoreType.REGULAR((8,)), dma((2, slots)), dma((2, slots)),
            dma, dma, dma((slots,)), dma((slots,)), dma, dma,
        ],
        compiler_params=pltpu.CompilerParams(collective_id=0, has_side_effects=True),
        name="cycle",
    )(increment, trajectory, *tables, correlation)


def solution(mesh):
    split_spec = P("tm", None, "space", None)
    return jax.shard_map(
        body,
        mesh=mesh,
        in_specs=(split_spec, split_spec, P(), P(), P(), P()),
        out_specs=split_spec,
        check_vma=False,
    )
```

```python
import functools

import jax
import jax.numpy as jnp
import numpy as np
from jax import lax
from jax.experimental import pallas as pl
from jax.experimental.pallas import tpu as pltpu
from jax.sharding import PartitionSpec as P

MESH = pl.DeviceIdType.MESH
F32, BF16 = jnp.float32, jnp.bfloat16
VMEM = pl.BlockSpec(memory_space=pltpu.VMEM)
HBM = pl.BlockSpec(memory_space=pl.ANY)

ROWS, FIELDS, CHANNELS = 8, 4, 32
PAIR = 2 * FIELDS
TAPS = 48
BIAS = 36
HALVES = ((-3, 3), (-1, 3))


def tap(a, b, f):
    return (a * 3 + b) * FIELDS + f


def selections():
    wide = np.zeros((4, 2 * TAPS, 28 * PAIR), np.float32)
    narrow = np.zeros((2, 2 * TAPS, 20 * PAIR), np.float32)
    for table, pairs in ((wide, 3), (narrow, 2)):
        third = pairs * 3 * PAIR
        for i in range(table.shape[0]):
            table[i, BIAS, 3 * third] = 1.0
            table[i, TAPS + BIAS, 3 * third + 1] = 1.0
            for k in range(pairs):
                for b in range(3):
                    for f in range(FIELDS):
                        for r in range(2):
                            a = 2 * k + r - i
                            if 0 <= a < 3:
                                line = (k * 3 + b) * PAIR + 2 * f + r
                                table[i, tap(a, b, f), line] = 1.0
                                table[i, tap(a, b, f), third + line] = 1.0
                                table[i, TAPS + tap(a, b, f), 2 * third + line] = 1.0
    out = np.zeros((2, 9 * PAIR, 4 * TAPS), np.float32)
    for k in range(3):
        for b in range(3):
            for f in range(FIELDS):
                for r in range(2):
                    for a in range(3):
                        i = 2 * k + r + a
                        out[i // 4, (k * 3 + b) * PAIR + 2 * f + r, i % 4 * TAPS + tap(a, b, f)] = 1.0
    return wide, narrow, out


def far_first(wide, deep):
    offsets = [(p, q) for p in range(wide) for q in range(deep) if p or q]
    hops = lambda n, size: min(n, size - n)
    return sorted(offsets, key=lambda o: (-hops(o[0], wide) - hops(o[1], deep), -hops(o[1], deep), o))


def split(x):
    high = x.astype(BF16)
    return high, (x - high.astype(F32)).astype(BF16)


def dot(a, b):
    return jnp.dot(a, b, preferred_element_type=F32)


def cycle_kernel(
    inc_hbm, traj_hbm, *refs,
):
    count = 7
    tables_hbm, corr, refs = refs[:count], refs[count], refs[count + 1 :]
    out, tables, refs = refs[0], refs[1 : count + 1], refs[count + 1 :]
    cycle(inc_hbm, traj_hbm, tables_hbm, corr, out, tables, *refs)


def cycle(
    inc_hbm, traj_hbm, tables_hbm, corr, out, tables,
    inc, traj, up, down, top, bot,
    taps_in, taps_out, t1, t1n, t2_first, t2_second,
    ones, xs, hh, hl, fore, before, rows, cols, results, back, cmat,
    in_sem, table_sem, c_sem, met, halo_send, halo_recv, nb_send, nb_recv, f_send, f_recv, b_send, b_recv,
):
    slots, nx = inc.shape[0], inc.shape[3]
    quarter = nx // 128
    depth = lax.axis_size("tm")
    width = depth // FIELDS
    me = lax.axis_index("tm")
    my_field, my_row = lax.div(me, width), lax.rem(me, width)
    place = lax.axis_index("space")
    last = lax.axis_size("space") - 1
    order = [slots - 1] + list(range(slots - 1))

    barrier = pltpu.get_barrier_semaphore()

    fields = [my_field] + [lax.rem(my_field + p, FIELDS) for p in range(1, FIELDS)]
    strips = [my_row] + [lax.rem(my_row + p, width) for p in range(1, width)]
    peers = [(fields[p], strips[q]) for p, q in far_first(FIELDS, width)]

    def device(peer):
        return {"tm": peer[0] * width + peer[1]}

    beside = [(my_field, strips[q]) for q in (2, -2)]
    close = [(my_field, strips[q]) for q in (1, -1)]
    across = [(fields[p], my_row) for p in range(1, FIELDS)]

    def say(sem, devices):
        for d in devices:
            pl.semaphore_signal(sem, inc=1, device_id=device(d), device_id_type=MESH)

    w_in, w_bias, w_out, pick_wide, pick_narrow, pick_out, perm = tables

    @pl.when(place > 0)
    def _():
        pl.semaphore_signal(barrier, inc=1, device_id={"space": place - 1}, device_id_type=MESH)

    @pl.when(place < last)
    def _():
        pl.semaphore_signal(barrier, inc=1, device_id={"space": place + 1}, device_id_type=MESH)

    def inputs(j):
        return (
            pltpu.make_async_copy(traj_hbm.at[j], traj.at[j], in_sem.at[0, j]),
            pltpu.make_async_copy(inc_hbm.at[j], inc.at[j], in_sem.at[1, j]),
        )

    say(barrier, beside + across + close)
    for j in order:
        for copy in inputs(j):
            copy.start()

    table_copies = [pltpu.make_async_copy(*x, table_sem.at[n]) for n, x in enumerate(zip(tables_hbm, tables))]
    for copy in table_copies:
        copy.start()
    c_copy = pltpu.make_async_copy(corr.at[my_field], cmat, c_sem)
    c_copy.start()

    def pack(j):
        for array, source in enumerate((traj, inc)):
            for f in range(FIELDS):
                for half, target in enumerate((up, down)):
                    for k in range(2):
                        r = 4 * half + 2 * k
                        target[j, array, PAIR * k + 2 * f : PAIR * k + 2 * f + 2, :] = source[j, f, r : r + 2, :]

    def to_next(j):
        return pltpu.make_async_remote_copy(
            down.at[j], top.at[j], halo_send.at[0, j], halo_recv.at[0, j],
            device_id={"space": place + 1}, device_id_type=MESH,
        )

    def to_previous(j):
        return pltpu.make_async_remote_copy(
            up.at[j], bot.at[j], halo_send.at[1, j], halo_recv.at[1, j],
            device_id={"space": place - 1}, device_id_type=MESH,
        )

    for n, j in enumerate(order):
        for copy in inputs(j):
            copy.wait()
        pack(j)
        if n == 0:
            pl.semaphore_wait(barrier, len(beside + across + close) + jnp.minimum(place, 1) + jnp.minimum(last - place, 1))
            say(met.at[0], beside)

        @pl.when(place < last)
        def _():
            to_next(j).start()

        @pl.when(place > 0)
        def _():
            to_previous(j).start()

    for copy in table_copies:
        copy.wait()

    taps_in[...] = jnp.zeros_like(taps_in)
    taps_out[...] = jnp.zeros_like(taps_out)
    for a in range(3):
        for b in range(3):
            at = tap(a, b, 0)
            taps_in[at : at + FIELDS, :CHANNELS] = w_in[a, b]
            w = 0.5 * w_out[a, b]
            for q in range(4):
                taps_out[q * TAPS + at : q * TAPS + at + FIELDS, q * CHANNELS : q * CHANNELS + CHANNELS] = w
    taps_in[BIAS : BIAS + 1, :CHANNELS] = w_bias[...]
    w = taps_in[:TAPS, :]
    high = w.astype(BF16).astype(F32)
    taps_in[:TAPS, :] = high
    taps_in[TAPS : 2 * TAPS, :] = w - high
    w = jnp.transpose(taps_in[...])[:CHANNELS]
    w = w[:, : 2 * TAPS].astype(BF16)
    for i in range(4):
        t1[CHANNELS * i : CHANNELS * i + CHANNELS, :] = dot(w, pick_wide[i]).astype(BF16)
    for i in range(2):
        t1n[CHANNELS * i : CHANNELS * i + CHANNELS, :] = dot(w, pick_narrow[i]).astype(BF16)
    lane_row = lax.shift_right_logical(lax.broadcasted_iota(jnp.int32, (1, 128), 1), 5) + place * ROWS
    for n, part in enumerate(split(taps_out[...])):
        for g in range(2):
            x = dot(pick_out[g], part)
            for step_id, target in enumerate((t2_first, t2_second)):
                lines = target.shape[1] // 2
                for half in range(2):
                    row = lane_row + (HALVES[step_id][half] + 4 * g)
                    keep = jnp.where((row >= 0) & (row < (last + 1) * ROWS), x[:lines], 0.0)
                    target[half, n * lines : n * lines + lines, 128 * g : 128 * g + 128] = keep.astype(BF16)

    @pl.when(place == 0)
    def _():
        top[...] = jnp.zeros_like(top)

    @pl.when(place == last)
    def _():
        bot[...] = jnp.zeros_like(bot)

    pl.semaphore_wait(met.at[0], len(beside))
    say(met.at[1], across)

    column = lax.broadcasted_iota(jnp.int32, (1, 128), 1)
    first, final = column == 0, column == 127

    def from_left(x):
        y = pltpu.roll(x, 1, 1)
        return jnp.concatenate([jnp.where(first, 0.0, y[:, :128]), y[:, 128:]], axis=1)

    def from_right(x):
        y = pltpu.roll(x, nx - 1, 1)
        return jnp.concatenate([y[:, : nx - 128], jnp.where(final, 0.0, y[:, nx - 128 :])], axis=1)

    ones[...] = jnp.where(
        (lax.broadcasted_iota(jnp.int32, ones.shape, 0) < 2)
        & (lax.broadcasted_iota(jnp.int32, ones.shape, 1) < nx),
        1.0,
        0.0,
    )

    def step(state, step_id):
        pairs = len(state[0])
        outs = pairs - 2
        mids = 2 * outs + 2
        highs, lows = [], []
        for k in range(pairs):
            high, low = [], []
            for array in range(2):
                x = state[array][k]
                x = jnp.concatenate([from_left(x), x, from_right(x)], axis=0)
                h = x.astype(BF16).astype(F32)
                high.append(h)
                low.append(x - h)
            highs.append(jnp.concatenate(high, axis=1))
            lows.append(jnp.concatenate(low, axis=1))
        spans = [(g, 3) for g in range(0, pairs - 2, 2)] + [(pairs - 2, 2)]
        for g, n in spans:
            high = highs[g : g + n]
            pad = [ones[:PAIR]] if n == 3 else [ones[...]]
            value = jnp.concatenate(high + lows[g : g + n] + high + pad, axis=0).astype(BF16)
            xs[g // 2, : value.shape[0], :] = value
        for n in range(0, nx, 256):
            s, t = slice(n, n + 256), slice(nx + n, nx + n + 256)
            at = 0
            for g, count in spans:
                table, many = (t1, 4) if count == 3 else (t1n, 2)
                depth_in = table.shape[1]
                zs = dot(table[...], xs[g // 2, :depth_in, s])
                zt = dot(table[...], xs[g // 2, :depth_in, t])
                h = jnp.tanh(zs)
                slope = (1.0 - h * h) * zt
                lines = slice(at, at + many * CHANNELS)
                hh[lines, s], hl[lines, s] = split(h)
                hh[lines, t], hl[lines, t] = split(slope)
                at += many * CHANNELS
        new = [[], []]
        wide, deep = outs // 2, (outs + 2) * CHANNELS
        table = (t2_first, t2_second)[step_id]
        for array in range(2):
            lane = slice(array * nx, array * nx + nx)
            for half in range(2):
                start = half * outs * CHANNELS
                lines = 3 * PAIR * wide
                both = dot(table[half, :, :deep], hh[start : start + deep, lane])
                taps = both[:lines] + both[lines:] + dot(table[half, :lines, :deep], hl[start : start + deep, lane])
                for k in range(wide):
                    left, middle, right = (taps[PAIR * n : PAIR * n + PAIR] for n in range(3 * k, 3 * k + 3))
                    new[array].append(state[array][half * wide + k + 1] + (from_left(left) + middle + from_right(right)))
        return new

    def line_of(peer):
        f, r = peer
        return lax.div(r, 2) * PAIR + 2 * f + lax.rem(r, 2)

    def send_residual(j, value):
        lines = rows.reshape(slots * depth * quarter, 128)
        for q in range(quarter):
            lines[pl.ds(j * depth * quarter + q, depth, stride=quarter), :] = value[:, 128 * q : 128 * q + 128]
        for peer in peers:
            pltpu.make_async_remote_copy(
                rows.at[j, line_of(peer)], cols.at[j, me], f_send.at[j], f_recv.at[j],
                device_id=device(peer), device_id_type=MESH,
            ).start()
        pltpu.make_async_copy(rows.at[j, line_of((my_field, my_row))], cols.at[j, me], f_recv.at[j]).start()

    def increment_lines(j):
        return jnp.concatenate([up[j, 1], down[j, 1]], axis=0)

    after = lax.rem(me + 1, depth)
    to_after = pltpu.make_async_remote_copy(fore, before, nb_send, nb_recv, device_id={"tm": after}, device_id_type=MESH)

    @pl.loop(0, slots)
    def _(i):
        slot = lax.rem(i + slots - 1, slots)

        @pl.when(place > 0)
        def _():
            to_next(slot).wait_recv()

        @pl.when(place < last)
        def _():
            to_previous(slot).wait_recv()

        state = []
        for array in range(2):
            parts = [x[slot, array] for x in (top, up, down, bot)]
            state.append([x[PAIR * k : PAIR * k + PAIR] for x in parts for k in range(2)])
        state = step(state, 0)
        for array in range(2):
            state[array][0] = jnp.where(place > 0, state[array][0], 0.0)
            state[array][-1] = jnp.where(place < last, state[array][-1], 0.0)

        state = step(state, 1)
        forecast = jnp.concatenate(state[1], axis=0)

        @pl.when(i == 0)
        def _():
            fore[...] = forecast
            pl.semaphore_wait(met.at[1], len(across))
            to_after.start()

        @pl.when(i > 0)
        def _():
            send_residual(slot + 1, increment_lines(slot + 1) - forecast)

        @pl.when(i == slots - 2)
        def _():
            to_after.wait()
            earlier = jnp.where(me == 0, 0.0, before[...])
            send_residual(0, increment_lines(0) - earlier)


    c_copy.wait()
    ch, cl = split(cmat[...])
    ch = dot(ch, perm[...]).astype(BF16)
    cl = dot(cl, perm[...]).astype(BF16)
    for j in range(slots):
        pltpu.make_async_copy(cols.at[j], cols.at[j], f_recv.at[j]).wait()
    received = cols.reshape(slots * depth * quarter, 128)
    sums = results.reshape(slots * depth * quarter, 128)
    vh, vl = split(jnp.concatenate([received[pl.ds(q, slots * depth, stride=quarter), :] for q in range(quarter)], axis=1))
    both = dot(jnp.concatenate([ch, cl], axis=0), vh)
    total = both[: slots * depth] + both[slots * depth :] + dot(ch, vl)
    for q in range(quarter):
        sums[pl.ds(q, slots * depth, stride=quarter), :] = total[:, 128 * q : 128 * q + 128]
    mine = pl.ds(me * slots, slots)
    for peer in peers:
        pltpu.make_async_remote_copy(
            results.at[pl.ds((peer[0] * width + peer[1]) * slots, slots)], back.at[mine], b_send, b_recv,
            device_id=device(peer), device_id_type=MESH,
        ).start()
    pltpu.make_async_copy(results.at[mine], back.at[mine], b_recv).start()

    pltpu.make_async_copy(back, back, b_recv).wait()
    lines = back.reshape(depth * slots * quarter, 128)
    for j in range(slots):
        for f in range(FIELDS):
            for q in range(quarter):
                out[j, f, :, 128 * q : 128 * q + 128] = lines[
                    pl.ds((f * width * slots + j) * quarter + q, ROWS, stride=slots * quarter), :
                ]
    rest = pl.ds(0, (depth - 1) * slots)
    pltpu.make_async_copy(results.at[rest], results.at[rest], b_send).wait()
    for j in range(slots):
        pltpu.make_async_copy(rows.at[j, pl.ds(0, depth - 1)], rows.at[j, pl.ds(0, depth - 1)], f_send.at[j]).wait()

        @pl.when(place < last)
        def _():
            to_next(j).wait_send()

        @pl.when(place > 0)
        def _():
            to_previous(j).wait_send()


def body(increment, trajectory, input_weight, bias, output_weight, correlation):
    slots, fields, rows, nx = increment.shape
    pick_wide, pick_narrow, pick_out = (jnp.asarray(x, BF16) for x in selections())
    depth = lax.axis_size("tm")
    time = correlation.shape[1]
    perm = np.zeros((time, time), np.float32)
    for e in range(depth):
        for j in range(slots):
            perm[e * slots + j, j * depth + e] = 1.0
    tables = (
        jnp.transpose(input_weight, (2, 3, 1, 0)), bias[None, :], jnp.transpose(output_weight, (2, 3, 0, 1)),
        pick_wide, pick_narrow, pick_out, jnp.asarray(perm, BF16),
    )
    local = increment.shape
    halo = (slots, 2, 2 * PAIR, nx)
    hidden = (14 * CHANNELS, 2 * nx)
    message = (slots, depth, nx // 128, 128)
    dma = pltpu.SemaphoreType.DMA
    return pl.pallas_call(
        cycle_kernel,
        out_shape=pltpu.VMEM(local, F32),
        in_specs=[HBM] * 10,
        out_specs=VMEM,
        scratch_shapes=[pltpu.VMEM(x.shape, x.dtype) for x in tables]
        + [
            pltpu.VMEM(local, F32),
            pltpu.VMEM(local, F32),
            pltpu.VMEM(halo, F32),
            pltpu.VMEM(halo, F32),
            pltpu.VMEM(halo, F32),
            pltpu.VMEM(halo, F32),
            pltpu.VMEM((128, 128), F32),
            pltpu.VMEM((4 * TAPS, 128), F32),
            pltpu.VMEM((4 * CHANNELS, 28 * PAIR), BF16),
            pltpu.VMEM((2 * CHANNELS, 20 * PAIR), BF16),
            pltpu.VMEM((2, 18 * PAIR, 256), BF16),
            pltpu.VMEM((2, 12 * PAIR, 256), BF16),
            pltpu.VMEM((2 * PAIR, 2 * nx), F32),
            pltpu.VMEM((4, 28 * PAIR, 2 * nx), BF16),
            pltpu.VMEM(hidden, BF16),
            pltpu.VMEM(hidden, BF16),
            pltpu.VMEM((fields * rows, nx), F32),
            pltpu.VMEM((fields * rows, nx), F32),
            pltpu.VMEM(message, F32),
            pltpu.VMEM(message, F32),
            pltpu.VMEM((time, nx // 128, 128), F32),
            pltpu.VMEM((time, nx // 128, 128), F32),
            pltpu.VMEM((time, time), F32),
            dma((2, slots)), dma((len(tables),)), dma, pltpu.SemaphoreType.REGULAR((2,)), dma((2, slots)), dma((2, slots)),
            dma, dma, dma((slots,)), dma((slots,)), dma, dma,
        ],
        compiler_params=pltpu.CompilerParams(collective_id=0, has_side_effects=True),
        name="cycle",
    )(increment, trajectory, *tables, correlation)


def solution(mesh):
    split_spec = P("tm", None, "space", None)
    return jax.shard_map(
        body,
        mesh=mesh,
        in_specs=(split_spec, split_spec, P(), P(), P(), P()),
        out_specs=split_spec,
        check_vma=False,
    )
```

```python
import functools

import jax
import jax.numpy as jnp
import numpy as np
from jax import lax
from jax.experimental import pallas as pl
from jax.experimental.pallas import tpu as pltpu
from jax.sharding import PartitionSpec as P

MESH = pl.DeviceIdType.MESH
F32, BF16 = jnp.float32, jnp.bfloat16
VMEM = pl.BlockSpec(memory_space=pltpu.VMEM)
HBM = pl.BlockSpec(memory_space=pl.ANY)

ROWS, FIELDS, CHANNELS = 8, 4, 32
PAIR = 2 * FIELDS
TAPS = 48
BIAS = 36
HALVES = ((-3, 3), (-1, 3))


def tap(a, b, f):
    return (a * 3 + b) * FIELDS + f


def selections():
    wide = np.zeros((4, 2 * TAPS, 28 * PAIR), np.float32)
    narrow = np.zeros((2, 2 * TAPS, 20 * PAIR), np.float32)
    for table, pairs in ((wide, 3), (narrow, 2)):
        third = pairs * 3 * PAIR
        for i in range(table.shape[0]):
            table[i, BIAS, 3 * third] = 1.0
            table[i, TAPS + BIAS, 3 * third + 1] = 1.0
            for k in range(pairs):
                for b in range(3):
                    for f in range(FIELDS):
                        for r in range(2):
                            a = 2 * k + r - i
                            if 0 <= a < 3:
                                line = (k * 3 + b) * PAIR + 2 * f + r
                                table[i, tap(a, b, f), line] = 1.0
                                table[i, tap(a, b, f), third + line] = 1.0
                                table[i, TAPS + tap(a, b, f), 2 * third + line] = 1.0
    out = np.zeros((2, 9 * PAIR, 4 * TAPS), np.float32)
    for k in range(3):
        for b in range(3):
            for f in range(FIELDS):
                for r in range(2):
                    for a in range(3):
                        i = 2 * k + r + a
                        out[i // 4, (k * 3 + b) * PAIR + 2 * f + r, i % 4 * TAPS + tap(a, b, f)] = 1.0
    return wide, narrow, out


def far_first(wide, deep):
    offsets = [(p, q) for p in range(wide) for q in range(deep) if p or q]
    hops = lambda n, size: min(n, size - n)
    return sorted(offsets, key=lambda o: (-hops(o[0], wide) - hops(o[1], deep), -hops(o[1], deep), o))


def split(x):
    high = x.astype(BF16)
    return high, (x - high.astype(F32)).astype(BF16)


def dot(a, b):
    return jnp.dot(a, b, preferred_element_type=F32)


def cycle_kernel(
    inc_hbm, traj_hbm, *refs,
):
    count = 7
    tables_hbm, corr, refs = refs[:count], refs[count], refs[count + 1 :]
    out, tables, refs = refs[0], refs[1 : count + 1], refs[count + 1 :]
    cycle(inc_hbm, traj_hbm, tables_hbm, corr, out, tables, *refs)


def cycle(
    inc_hbm, traj_hbm, tables_hbm, corr, out, tables,
    inc, traj, up, down, top, bot,
    taps_in, taps_out, t1, t1n, t2_first, t2_second,
    ones, xs, hh, hl, rows_two, cols_two, rows, cols, results, back, cmat,
    in_sem, table_sem, c_sem, met, halo_send, halo_recv, f_send, f_recv, b_send, b_recv,
):
    slots, nx = inc.shape[0], inc.shape[3]
    quarter = nx // 128
    depth = lax.axis_size("tm")
    width = depth // FIELDS
    me = lax.axis_index("tm")
    my_field, my_row = lax.div(me, width), lax.rem(me, width)
    place = lax.axis_index("space")
    last = lax.axis_size("space") - 1
    order = range(slots)

    barrier = pltpu.get_barrier_semaphore()

    fields = [my_field] + [lax.rem(my_field + p, FIELDS) for p in range(1, FIELDS)]
    strips = [my_row] + [lax.rem(my_row + p, width) for p in range(1, width)]
    peers = [(fields[p], strips[q]) for p, q in far_first(FIELDS, width)]

    def device(peer):
        return {"tm": peer[0] * width + peer[1]}

    beside = [(my_field, strips[q]) for q in (2, -2)]
    close = [(my_field, strips[q]) for q in (1, -1)]
    across = [(fields[p], my_row) for p in range(1, FIELDS)]

    def say(sem, devices):
        for d in devices:
            pl.semaphore_signal(sem, inc=1, device_id=device(d), device_id_type=MESH)

    w_in, w_bias, w_out, pick_wide, pick_narrow, pick_out, perm = tables

    @pl.when(place > 0)
    def _():
        pl.semaphore_signal(barrier, inc=1, device_id={"space": place - 1}, device_id_type=MESH)

    @pl.when(place < last)
    def _():
        pl.semaphore_signal(barrier, inc=1, device_id={"space": place + 1}, device_id_type=MESH)

    def inputs(j):
        return (
            pltpu.make_async_copy(traj_hbm.at[j], traj.at[j], in_sem.at[0, j]),
            pltpu.make_async_copy(inc_hbm.at[j], inc.at[j], in_sem.at[1, j]),
        )

    say(barrier, beside + across + close)
    for j in order:
        for copy in inputs(j):
            copy.start()

    table_copies = [pltpu.make_async_copy(*x, table_sem.at[n]) for n, x in enumerate(zip(tables_hbm, tables))]
    for copy in table_copies:
        copy.start()
    c_copy = pltpu.make_async_copy(corr.at[my_field], cmat, c_sem)
    c_copy.start()

    def pack(j):
        for array, source in enumerate((traj, inc)):
            for f in range(FIELDS):
                for half, target in enumerate((up, down)):
                    for k in range(2):
                        r = 4 * half + 2 * k
                        target[j, array, PAIR * k + 2 * f : PAIR * k + 2 * f + 2, :] = source[j, f, r : r + 2, :]

    def to_next(j):
        return pltpu.make_async_remote_copy(
            down.at[j], top.at[j], halo_send.at[0, j], halo_recv.at[0, j],
            device_id={"space": place + 1}, device_id_type=MESH,
        )

    def to_previous(j):
        return pltpu.make_async_remote_copy(
            up.at[j], bot.at[j], halo_send.at[1, j], halo_recv.at[1, j],
            device_id={"space": place - 1}, device_id_type=MESH,
        )

    for n, j in enumerate(order):
        for copy in inputs(j):
            copy.wait()
        pack(j)
        if n == 0:
            pl.semaphore_wait(barrier, len(beside + across + close) + jnp.minimum(place, 1) + jnp.minimum(last - place, 1))
            say(met.at[0], beside)

        @pl.when(place < last)
        def _():
            to_next(j).start()

        @pl.when(place > 0)
        def _():
            to_previous(j).start()

    for copy in table_copies:
        copy.wait()

    taps_in[...] = jnp.zeros_like(taps_in)
    taps_out[...] = jnp.zeros_like(taps_out)
    for a in range(3):
        for b in range(3):
            at = tap(a, b, 0)
            taps_in[at : at + FIELDS, :CHANNELS] = w_in[a, b]
            w = 0.5 * w_out[a, b]
            for q in range(4):
                taps_out[q * TAPS + at : q * TAPS + at + FIELDS, q * CHANNELS : q * CHANNELS + CHANNELS] = w
    taps_in[BIAS : BIAS + 1, :CHANNELS] = w_bias[...]
    w = taps_in[:TAPS, :]
    high = w.astype(BF16).astype(F32)
    taps_in[:TAPS, :] = high
    taps_in[TAPS : 2 * TAPS, :] = w - high
    w = jnp.transpose(taps_in[...])[:CHANNELS]
    w = w[:, : 2 * TAPS].astype(BF16)
    for i in range(4):
        t1[CHANNELS * i : CHANNELS * i + CHANNELS, :] = dot(w, pick_wide[i]).astype(BF16)
    for i in range(2):
        t1n[CHANNELS * i : CHANNELS * i + CHANNELS, :] = dot(w, pick_narrow[i]).astype(BF16)
    lane_row = lax.shift_right_logical(lax.broadcasted_iota(jnp.int32, (1, 128), 1), 5) + place * ROWS
    for n, part in enumerate(split(taps_out[...])):
        for g in range(2):
            x = dot(pick_out[g], part)
            for step_id, target in enumerate((t2_first, t2_second)):
                lines = target.shape[1] // 2
                for half in range(2):
                    row = lane_row + (HALVES[step_id][half] + 4 * g)
                    keep = jnp.where((row >= 0) & (row < (last + 1) * ROWS), x[:lines], 0.0)
                    target[half, n * lines : n * lines + lines, 128 * g : 128 * g + 128] = keep.astype(BF16)

    @pl.when(place == 0)
    def _():
        top[...] = jnp.zeros_like(top)

    @pl.when(place == last)
    def _():
        bot[...] = jnp.zeros_like(bot)

    pl.semaphore_wait(met.at[0], len(beside))
    say(met.at[1], across)

    column = lax.broadcasted_iota(jnp.int32, (1, 128), 1)
    first, final = column == 0, column == 127

    def from_left(x):
        y = pltpu.roll(x, 1, 1)
        return jnp.concatenate([jnp.where(first, 0.0, y[:, :128]), y[:, 128:]], axis=1)

    def from_right(x):
        y = pltpu.roll(x, nx - 1, 1)
        return jnp.concatenate([y[:, : nx - 128], jnp.where(final, 0.0, y[:, nx - 128 :])], axis=1)

    ones[...] = jnp.where(
        (lax.broadcasted_iota(jnp.int32, ones.shape, 0) < 2)
        & (lax.broadcasted_iota(jnp.int32, ones.shape, 1) < nx),
        1.0,
        0.0,
    )

    def step(state, step_id):
        pairs = len(state[0])
        outs = pairs - 2
        mids = 2 * outs + 2
        highs, lows = [], []
        for k in range(pairs):
            high, low = [], []
            for array in range(2):
                x = state[array][k]
                x = jnp.concatenate([from_left(x), x, from_right(x)], axis=0)
                h = x.astype(BF16).astype(F32)
                high.append(h)
                low.append(x - h)
            highs.append(jnp.concatenate(high, axis=1))
            lows.append(jnp.concatenate(low, axis=1))
        spans = [(g, 3) for g in range(0, pairs - 2, 2)] + [(pairs - 2, 2)]
        for g, n in spans:
            high = highs[g : g + n]
            pad = [ones[:PAIR]] if n == 3 else [ones[...]]
            value = jnp.concatenate(high + lows[g : g + n] + high + pad, axis=0).astype(BF16)
            xs[g // 2, : value.shape[0], :] = value
        for n in range(0, nx, 256):
            s, t = slice(n, n + 256), slice(nx + n, nx + n + 256)
            at = 0
            for g, count in spans:
                table, many = (t1, 4) if count == 3 else (t1n, 2)
                depth_in = table.shape[1]
                zs = dot(table[...], xs[g // 2, :depth_in, s])
                zt = dot(table[...], xs[g // 2, :depth_in, t])
                h = jnp.tanh(zs)
                slope = (1.0 - h * h) * zt
                lines = slice(at, at + many * CHANNELS)
                hh[lines, s], hl[lines, s] = split(h)
                hh[lines, t], hl[lines, t] = split(slope)
                at += many * CHANNELS
        new = [[], []]
        wide, deep = outs // 2, (outs + 2) * CHANNELS
        table = (t2_first, t2_second)[step_id]
        for array in range(2):
            lane = slice(array * nx, array * nx + nx)
            for half in range(2):
                start = half * outs * CHANNELS
                lines = 3 * PAIR * wide
                both = dot(table[half, :, :deep], hh[start : start + deep, lane])
                taps = both[:lines] + both[lines:] + dot(table[half, :lines, :deep], hl[start : start + deep, lane])
                for k in range(wide):
                    left, middle, right = (taps[PAIR * n : PAIR * n + PAIR] for n in range(3 * k, 3 * k + 3))
                    new[array].append(state[array][half * wide + k + 1] + (from_left(left) + middle + from_right(right)))
        return new

    def line_of(peer):
        f, r = peer
        return lax.div(r, 2) * PAIR + 2 * f + lax.rem(r, 2)

    def send_lines(phase, outgoing, incoming):
        for peer in peers:
            pltpu.make_async_remote_copy(
                outgoing.at[line_of(peer)], incoming.at[me], f_send.at[phase], f_recv.at[phase],
                device_id=device(peer), device_id_type=MESH,
            ).start()
        own = outgoing.at[line_of((my_field, my_row))]
        pltpu.make_async_copy(own, incoming.at[me], f_recv.at[phase]).start()

    def increment_lines(j):
        return jnp.concatenate([up[j, 1], down[j, 1]], axis=0)

    @pl.loop(0, slots)
    def _(i):
        slot = i

        @pl.when(place > 0)
        def _():
            to_next(slot).wait_recv()

        @pl.when(place < last)
        def _():
            to_previous(slot).wait_recv()

        state = []
        for array in range(2):
            parts = [x[slot, array] for x in (top, up, down, bot)]
            state.append([x[PAIR * k : PAIR * k + PAIR] for x in parts for k in range(2)])
        state = step(state, 0)
        for array in range(2):
            state[array][0] = jnp.where(place > 0, state[array][0], 0.0)
            state[array][-1] = jnp.where(place < last, state[array][-1], 0.0)

        state = step(state, 1)
        forecast = jnp.concatenate(state[1], axis=0)

        @pl.when(i == 0)
        def _():
            pair = (increment_lines(0), increment_lines(1) - forecast)
            lines = rows_two.reshape(depth * 2 * quarter, 128)
            for n, value in enumerate(pair):
                for q in range(quarter):
                    lines[pl.ds(n * quarter + q, depth, stride=2 * quarter), :] = value[:, 128 * q : 128 * q + 128]
            pl.semaphore_wait(met.at[1], len(across))
            send_lines(0, rows_two, cols_two)

        @pl.when(i > 0)
        def _():
            following = increment_lines(jnp.minimum(i + 1, slots - 1))
            value = jnp.where(i < slots - 1, following, 0.0) - forecast
            lines = rows.reshape((slots - 1) * depth * quarter, 128)
            for q in range(quarter):
                lines[pl.ds((i - 1) * depth * quarter + q, depth, stride=quarter), :] = value[:, 128 * q : 128 * q + 128]
            send_lines(i, rows.at[i - 1], cols.at[i - 1])

    c_copy.wait()
    ch, cl = split(cmat[...])
    ch = dot(ch, perm[...]).astype(BF16)
    cl = dot(cl, perm[...]).astype(BF16)
    two = cols_two.reshape(depth * 2 * quarter, 128)
    one = cols.reshape((slots - 1) * depth * quarter, 128)
    sums = results.reshape(slots * depth * quarter, 128)

    def received(x, start, stride):
        return jnp.concatenate([x[pl.ds(start + q, depth, stride=stride), :] for q in range(quarter)], axis=1)

    pltpu.make_async_copy(cols_two, cols_two, f_recv.at[0]).wait()
    values = [received(two, 0, 2 * quarter), received(two, quarter, 2 * quarter)]
    for n in range(slots - 1):
        pltpu.make_async_copy(cols.at[n], cols.at[n], f_recv.at[n + 1]).wait()
        values.append(received(one, n * depth * quarter, quarter))
    earlier = pltpu.roll(values.pop(), 1, 0)
    values[0] += jnp.where(lax.broadcasted_iota(jnp.int32, earlier.shape, 0) == 0, 0.0, earlier)
    vh, vl = split(jnp.concatenate(values, axis=0))
    both = dot(jnp.concatenate([ch, cl], axis=0), vh)
    total = both[: slots * depth] + both[slots * depth :] + dot(ch, vl)
    for q in range(quarter):
        sums[pl.ds(q, slots * depth, stride=quarter), :] = total[:, 128 * q : 128 * q + 128]
    mine = pl.ds(me * slots, slots)
    for peer in peers:
        pltpu.make_async_remote_copy(
            results.at[pl.ds((peer[0] * width + peer[1]) * slots, slots)], back.at[mine], b_send, b_recv,
            device_id=device(peer), device_id_type=MESH,
        ).start()
    pltpu.make_async_copy(results.at[mine], back.at[mine], b_recv).start()

    pltpu.make_async_copy(back, back, b_recv).wait()
    lines = back.reshape(depth * slots * quarter, 128)
    for j in range(slots):
        for f in range(FIELDS):
            for q in range(quarter):
                out[j, f, :, 128 * q : 128 * q + 128] = lines[
                    pl.ds((f * width * slots + j) * quarter + q, ROWS, stride=slots * quarter), :
                ]
    rest = pl.ds(0, (depth - 1) * slots)
    pltpu.make_async_copy(results.at[rest], results.at[rest], b_send).wait()
    others = pl.ds(0, depth - 1)
    pltpu.make_async_copy(rows_two.at[others], rows_two.at[others], f_send.at[0]).wait()
    for n in range(slots - 1):
        pltpu.make_async_copy(rows.at[n, others], rows.at[n, others], f_send.at[n + 1]).wait()
    for j in range(slots):

        @pl.when(place < last)
        def _():
            to_next(j).wait_send()

        @pl.when(place > 0)
        def _():
            to_previous(j).wait_send()


def body(increment, trajectory, input_weight, bias, output_weight, correlation):
    slots, fields, rows, nx = increment.shape
    pick_wide, pick_narrow, pick_out = (jnp.asarray(x, BF16) for x in selections())
    depth = lax.axis_size("tm")
    time = correlation.shape[1]
    perm = np.zeros((time, time), np.float32)
    for e in range(depth):
        for j in range(slots):
            perm[e * slots + j, j * depth + e] = 1.0
    tables = (
        jnp.transpose(input_weight, (2, 3, 1, 0)), bias[None, :], jnp.transpose(output_weight, (2, 3, 0, 1)),
        pick_wide, pick_narrow, pick_out, jnp.asarray(perm, BF16),
    )
    local = increment.shape
    halo = (slots, 2, 2 * PAIR, nx)
    hidden = (14 * CHANNELS, 2 * nx)
    message = (slots - 1, depth, nx // 128, 128)
    dma = pltpu.SemaphoreType.DMA
    return pl.pallas_call(
        cycle_kernel,
        out_shape=pltpu.VMEM(local, F32),
        in_specs=[HBM] * 10,
        out_specs=VMEM,
        scratch_shapes=[pltpu.VMEM(x.shape, x.dtype) for x in tables]
        + [
            pltpu.VMEM(local, F32),
            pltpu.VMEM(local, F32),
            pltpu.VMEM(halo, F32),
            pltpu.VMEM(halo, F32),
            pltpu.VMEM(halo, F32),
            pltpu.VMEM(halo, F32),
            pltpu.VMEM((128, 128), F32),
            pltpu.VMEM((4 * TAPS, 128), F32),
            pltpu.VMEM((4 * CHANNELS, 28 * PAIR), BF16),
            pltpu.VMEM((2 * CHANNELS, 20 * PAIR), BF16),
            pltpu.VMEM((2, 18 * PAIR, 256), BF16),
            pltpu.VMEM((2, 12 * PAIR, 256), BF16),
            pltpu.VMEM((2 * PAIR, 2 * nx), F32),
            pltpu.VMEM((4, 28 * PAIR, 2 * nx), BF16),
            pltpu.VMEM(hidden, BF16),
            pltpu.VMEM(hidden, BF16),
            pltpu.VMEM((depth, 2, nx // 128, 128), F32),
            pltpu.VMEM((depth, 2, nx // 128, 128), F32),
            pltpu.VMEM(message, F32),
            pltpu.VMEM(message, F32),
            pltpu.VMEM((time, nx // 128, 128), F32),
            pltpu.VMEM((time, nx // 128, 128), F32),
            pltpu.VMEM((time, time), F32),
            dma((2, slots)), dma((len(tables),)), dma, pltpu.SemaphoreType.REGULAR((2,)), dma((2, slots)), dma((2, slots)),
            dma((slots,)), dma((slots,)), dma, dma,
        ],
        compiler_params=pltpu.CompilerParams(collective_id=0, has_side_effects=True),
        name="cycle",
    )(increment, trajectory, *tables, correlation)


def solution(mesh):
    split_spec = P("tm", None, "space", None)
    return jax.shard_map(
        body,
        mesh=mesh,
        in_specs=(split_spec, split_spec, P(), P(), P(), P()),
        out_specs=split_spec,
        check_vma=False,
    )
```

```python
import functools

import jax
import jax.numpy as jnp
import numpy as np
from jax import lax
from jax.experimental import pallas as pl
from jax.experimental.pallas import tpu as pltpu
from jax.sharding import PartitionSpec as P

MESH = pl.DeviceIdType.MESH
F32, BF16 = jnp.float32, jnp.bfloat16
VMEM = pl.BlockSpec(memory_space=pltpu.VMEM)
HBM = pl.BlockSpec(memory_space=pl.ANY)

ROWS, FIELDS, CHANNELS = 8, 4, 32
PAIR = 2 * FIELDS
TAPS = 48
BIAS = 36
HALVES = ((-3, 3), (-1, 3))


def tap(a, b, f):
    return (a * 3 + b) * FIELDS + f


def selections():
    wide = np.zeros((4, 2 * TAPS, 28 * PAIR), np.float32)
    narrow = np.zeros((2, 2 * TAPS, 20 * PAIR), np.float32)
    for table, pairs in ((wide, 3), (narrow, 2)):
        third = pairs * 3 * PAIR
        for i in range(table.shape[0]):
            table[i, BIAS, 3 * third] = 1.0
            table[i, TAPS + BIAS, 3 * third + 1] = 1.0
            for k in range(pairs):
                for b in range(3):
                    for f in range(FIELDS):
                        for r in range(2):
                            a = 2 * k + r - i
                            if 0 <= a < 3:
                                line = (k * 3 + b) * PAIR + 2 * f + r
                                table[i, tap(a, b, f), line] = 1.0
                                table[i, tap(a, b, f), third + line] = 1.0
                                table[i, TAPS + tap(a, b, f), 2 * third + line] = 1.0
    out = np.zeros((2, 9 * PAIR, 4 * TAPS), np.float32)
    for k in range(3):
        for b in range(3):
            for f in range(FIELDS):
                for r in range(2):
                    for a in range(3):
                        i = 2 * k + r + a
                        out[i // 4, (k * 3 + b) * PAIR + 2 * f + r, i % 4 * TAPS + tap(a, b, f)] = 1.0
    return wide, narrow, out


def far_first(wide, deep):
    offsets = [(p, q) for p in range(wide) for q in range(deep) if p or q]
    hops = lambda n, size: min(n, size - n)
    return sorted(offsets, key=lambda o: (-hops(o[0], wide) - hops(o[1], deep), -hops(o[1], deep), o))


def split(x):
    high = x.astype(BF16)
    return high, (x - high.astype(F32)).astype(BF16)


def dot(a, b):
    return jnp.dot(a, b, preferred_element_type=F32)


def cycle_kernel(
    inc_hbm, traj_hbm, *refs,
):
    count = 7
    tables_hbm, corr, refs = refs[:count], refs[count], refs[count + 1 :]
    out, tables, refs = refs[0], refs[1 : count + 1], refs[count + 1 :]
    cycle(inc_hbm, traj_hbm, tables_hbm, corr, out, tables, *refs)


def cycle(
    inc_hbm, traj_hbm, tables_hbm, corr, out, tables,
    inc, traj, up, down, top, bot,
    taps_in, taps_out, t1, t1n, t2_first, t2_second,
    ones, xs, hh, hl, rows_two, cols_two, rows, cols, results, partial, back, cmat,
    in_sem, table_sem, c_sem, met, halo_send, halo_recv, f_send, f_recv, b_send, b_recv,
):
    slots, nx = inc.shape[0], inc.shape[3]
    quarter = nx // 128
    depth = lax.axis_size("tm")
    width = depth // FIELDS
    me = lax.axis_index("tm")
    my_field, my_row = lax.div(me, width), lax.rem(me, width)
    place = lax.axis_index("space")
    last = lax.axis_size("space") - 1
    order = range(slots)

    barrier = pltpu.get_barrier_semaphore()

    fields = [my_field] + [lax.rem(my_field + p, FIELDS) for p in range(1, FIELDS)]
    strips = [my_row] + [lax.rem(my_row + p, width) for p in range(1, width)]
    peers = [(fields[p], strips[q]) for p, q in far_first(FIELDS, width)]

    def device(peer):
        return {"tm": peer[0] * width + peer[1]}

    beside = [(my_field, strips[q]) for q in (2, -2)]
    close = [(my_field, strips[q]) for q in (1, -1)]
    across = [(fields[p], my_row) for p in range(1, FIELDS)]

    def say(sem, devices):
        for d in devices:
            pl.semaphore_signal(sem, inc=1, device_id=device(d), device_id_type=MESH)

    w_in, w_bias, w_out, pick_wide, pick_narrow, pick_out, perm = tables

    @pl.when(place > 0)
    def _():
        pl.semaphore_signal(barrier, inc=1, device_id={"space": place - 1}, device_id_type=MESH)

    @pl.when(place < last)
    def _():
        pl.semaphore_signal(barrier, inc=1, device_id={"space": place + 1}, device_id_type=MESH)

    def inputs(j):
        return (
            pltpu.make_async_copy(traj_hbm.at[j], traj.at[j], in_sem.at[0, j]),
            pltpu.make_async_copy(inc_hbm.at[j], inc.at[j], in_sem.at[1, j]),
        )

    say(barrier, beside + across + close)
    for j in order:
        for copy in inputs(j):
            copy.start()

    table_copies = [pltpu.make_async_copy(*x, table_sem.at[n]) for n, x in enumerate(zip(tables_hbm, tables))]
    for copy in table_copies:
        copy.start()
    c_copy = pltpu.make_async_copy(corr.at[my_field], cmat, c_sem)
    c_copy.start()

    def pack(j):
        for array, source in enumerate((traj, inc)):
            for f in range(FIELDS):
                for half, target in enumerate((up, down)):
                    for k in range(2):
                        r = 4 * half + 2 * k
                        target[j, array, PAIR * k + 2 * f : PAIR * k + 2 * f + 2, :] = source[j, f, r : r + 2, :]

    def to_next(j):
        return pltpu.make_async_remote_copy(
            down.at[j], top.at[j], halo_send.at[0, j], halo_recv.at[0, j],
            device_id={"space": place + 1}, device_id_type=MESH,
        )

    def to_previous(j):
        return pltpu.make_async_remote_copy(
            up.at[j], bot.at[j], halo_send.at[1, j], halo_recv.at[1, j],
            device_id={"space": place - 1}, device_id_type=MESH,
        )

    for n, j in enumerate(order):
        for copy in inputs(j):
            copy.wait()
        pack(j)
        if n == 0:
            pl.semaphore_wait(barrier, len(beside + across + close) + jnp.minimum(place, 1) + jnp.minimum(last - place, 1))
            say(met.at[0], beside)

        @pl.when(place < last)
        def _():
            to_next(j).start()

        @pl.when(place > 0)
        def _():
            to_previous(j).start()

    for copy in table_copies:
        copy.wait()

    taps_in[...] = jnp.zeros_like(taps_in)
    taps_out[...] = jnp.zeros_like(taps_out)
    for a in range(3):
        for b in range(3):
            at = tap(a, b, 0)
            taps_in[at : at + FIELDS, :CHANNELS] = w_in[a, b]
            w = 0.5 * w_out[a, b]
            for q in range(4):
                taps_out[q * TAPS + at : q * TAPS + at + FIELDS, q * CHANNELS : q * CHANNELS + CHANNELS] = w
    taps_in[BIAS : BIAS + 1, :CHANNELS] = w_bias[...]
    w = taps_in[:TAPS, :]
    high = w.astype(BF16).astype(F32)
    taps_in[:TAPS, :] = high
    taps_in[TAPS : 2 * TAPS, :] = w - high
    w = jnp.transpose(taps_in[...])[:CHANNELS]
    w = w[:, : 2 * TAPS].astype(BF16)
    for i in range(4):
        t1[CHANNELS * i : CHANNELS * i + CHANNELS, :] = dot(w, pick_wide[i]).astype(BF16)
    for i in range(2):
        t1n[CHANNELS * i : CHANNELS * i + CHANNELS, :] = dot(w, pick_narrow[i]).astype(BF16)
    lane_row = lax.shift_right_logical(lax.broadcasted_iota(jnp.int32, (1, 128), 1), 5) + place * ROWS
    for n, part in enumerate(split(taps_out[...])):
        for g in range(2):
            x = dot(pick_out[g], part)
            for step_id, target in enumerate((t2_first, t2_second)):
                lines = target.shape[1] // 2
                for half in range(2):
                    row = lane_row + (HALVES[step_id][half] + 4 * g)
                    keep = jnp.where((row >= 0) & (row < (last + 1) * ROWS), x[:lines], 0.0)
                    target[half, n * lines : n * lines + lines, 128 * g : 128 * g + 128] = keep.astype(BF16)

    @pl.when(place == 0)
    def _():
        top[...] = jnp.zeros_like(top)

    @pl.when(place == last)
    def _():
        bot[...] = jnp.zeros_like(bot)

    pl.semaphore_wait(met.at[0], len(beside))
    say(met.at[1], across)

    column = lax.broadcasted_iota(jnp.int32, (1, 128), 1)
    first, final = column == 0, column == 127

    def from_left(x):
        y = pltpu.roll(x, 1, 1)
        return jnp.concatenate([jnp.where(first, 0.0, y[:, :128]), y[:, 128:]], axis=1)

    def from_right(x):
        y = pltpu.roll(x, nx - 1, 1)
        return jnp.concatenate([y[:, : nx - 128], jnp.where(final, 0.0, y[:, nx - 128 :])], axis=1)

    ones[...] = jnp.where(
        (lax.broadcasted_iota(jnp.int32, ones.shape, 0) < 2)
        & (lax.broadcasted_iota(jnp.int32, ones.shape, 1) < nx),
        1.0,
        0.0,
    )

    def step(state, step_id):
        pairs = len(state[0])
        outs = pairs - 2
        mids = 2 * outs + 2
        highs, lows = [], []
        for k in range(pairs):
            high, low = [], []
            for array in range(2):
                x = state[array][k]
                x = jnp.concatenate([from_left(x), x, from_right(x)], axis=0)
                h = x.astype(BF16).astype(F32)
                high.append(h)
                low.append(x - h)
            highs.append(jnp.concatenate(high, axis=1))
            lows.append(jnp.concatenate(low, axis=1))
        spans = [(g, 3) for g in range(0, pairs - 2, 2)] + [(pairs - 2, 2)]
        for g, n in spans:
            high = highs[g : g + n]
            pad = [ones[:PAIR]] if n == 3 else [ones[...]]
            value = jnp.concatenate(high + lows[g : g + n] + high + pad, axis=0).astype(BF16)
            xs[g // 2, : value.shape[0], :] = value
        for n in range(0, nx, 256):
            s, t = slice(n, n + 256), slice(nx + n, nx + n + 256)
            at = 0
            for g, count in spans:
                table, many = (t1, 4) if count == 3 else (t1n, 2)
                depth_in = table.shape[1]
                zs = dot(table[...], xs[g // 2, :depth_in, s])
                zt = dot(table[...], xs[g // 2, :depth_in, t])
                h = jnp.tanh(zs)
                slope = (1.0 - h * h) * zt
                lines = slice(at, at + many * CHANNELS)
                hh[lines, s], hl[lines, s] = split(h)
                hh[lines, t], hl[lines, t] = split(slope)
                at += many * CHANNELS
        new = [[], []]
        wide, deep = outs // 2, (outs + 2) * CHANNELS
        table = (t2_first, t2_second)[step_id]
        for array in range(2):
            lane = slice(array * nx, array * nx + nx)
            for half in range(2):
                start = half * outs * CHANNELS
                lines = 3 * PAIR * wide
                both = dot(table[half, :, :deep], hh[start : start + deep, lane])
                taps = both[:lines] + both[lines:] + dot(table[half, :lines, :deep], hl[start : start + deep, lane])
                for k in range(wide):
                    left, middle, right = (taps[PAIR * n : PAIR * n + PAIR] for n in range(3 * k, 3 * k + 3))
                    new[array].append(state[array][half * wide + k + 1] + (from_left(left) + middle + from_right(right)))
        return new

    def line_of(peer):
        f, r = peer
        return lax.div(r, 2) * PAIR + 2 * f + lax.rem(r, 2)

    def send_lines(phase, outgoing, incoming):
        for peer in peers:
            pltpu.make_async_remote_copy(
                outgoing.at[line_of(peer)], incoming.at[me], f_send.at[phase], f_recv.at[phase],
                device_id=device(peer), device_id_type=MESH,
            ).start()
        own = outgoing.at[line_of((my_field, my_row))]
        pltpu.make_async_copy(own, incoming.at[me], f_recv.at[phase]).start()

    def increment_lines(j):
        return jnp.concatenate([up[j, 1], down[j, 1]], axis=0)

    @pl.loop(0, slots)
    def _(i):
        slot = i

        @pl.when(place > 0)
        def _():
            to_next(slot).wait_recv()

        @pl.when(place < last)
        def _():
            to_previous(slot).wait_recv()

        state = []
        for array in range(2):
            parts = [x[slot, array] for x in (top, up, down, bot)]
            state.append([x[PAIR * k : PAIR * k + PAIR] for x in parts for k in range(2)])
        state = step(state, 0)
        for array in range(2):
            state[array][0] = jnp.where(place > 0, state[array][0], 0.0)
            state[array][-1] = jnp.where(place < last, state[array][-1], 0.0)

        state = step(state, 1)
        forecast = jnp.concatenate(state[1], axis=0)

        @pl.when(i == 0)
        def _():
            pair = (increment_lines(0), increment_lines(1) - forecast)
            lines = rows_two.reshape(depth * 2 * quarter, 128)
            for n, value in enumerate(pair):
                for q in range(quarter):
                    lines[pl.ds(n * quarter + q, depth, stride=2 * quarter), :] = value[:, 128 * q : 128 * q + 128]
            pl.semaphore_wait(met.at[1], len(across))
            send_lines(0, rows_two, cols_two)

        @pl.when(i > 0)
        def _():
            following = increment_lines(jnp.minimum(i + 1, slots - 1))
            value = jnp.where(i < slots - 1, following, 0.0) - forecast
            lines = rows.reshape((slots - 1) * depth * quarter, 128)
            for q in range(quarter):
                lines[pl.ds((i - 1) * depth * quarter + q, depth, stride=quarter), :] = value[:, 128 * q : 128 * q + 128]
            send_lines(i, rows.at[i - 1], cols.at[i - 1])

    c_copy.wait()
    ch, cl = split(cmat[...])
    both = jnp.concatenate([ch, cl], axis=0)
    both = dot(both, perm[...]).astype(BF16)
    time = slots * depth
    two = cols_two.reshape(depth * 2 * quarter, 128)
    one = cols.reshape((slots - 1) * depth * quarter, 128)
    sums = results.reshape(time * quarter, 128)

    def received(x, start, stride):
        return jnp.concatenate([x[pl.ds(start + q, depth, stride=stride), :] for q in range(quarter)], axis=1)

    def product(columns, values):
        vh, vl = split(values)
        x = dot(both[:, columns], vh)
        return x[:time] + x[time:] + dot(both[:time, columns], vl)

    pltpu.make_async_copy(cols_two, cols_two, f_recv.at[0]).wait()
    values = [received(two, 0, 2 * quarter), received(two, quarter, 2 * quarter)]
    for n in range(slots - 2):
        pltpu.make_async_copy(cols.at[n], cols.at[n], f_recv.at[n + 1]).wait()
        values.append(received(one, n * depth * quarter, quarter))
    partial[...] = product(slice(0, time), jnp.concatenate(values, axis=0))
    pltpu.make_async_copy(cols.at[slots - 2], cols.at[slots - 2], f_recv.at[slots - 1]).wait()
    total = partial[...] + product(slice(time, time + depth), received(one, (slots - 2) * depth * quarter, quarter))
    for q in range(quarter):
        sums[pl.ds(q, time, stride=quarter), :] = total[:, 128 * q : 128 * q + 128]
    mine = pl.ds(me * slots, slots)
    for peer in peers:
        pltpu.make_async_remote_copy(
            results.at[pl.ds((peer[0] * width + peer[1]) * slots, slots)], back.at[mine], b_send, b_recv,
            device_id=device(peer), device_id_type=MESH,
        ).start()
    pltpu.make_async_copy(results.at[mine], back.at[mine], b_recv).start()

    pltpu.make_async_copy(back, back, b_recv).wait()
    lines = back.reshape(depth * slots * quarter, 128)
    for j in range(slots):
        for f in range(FIELDS):
            for q in range(quarter):
                out[j, f, :, 128 * q : 128 * q + 128] = lines[
                    pl.ds((f * width * slots + j) * quarter + q, ROWS, stride=slots * quarter), :
                ]
    rest = pl.ds(0, (depth - 1) * slots)
    pltpu.make_async_copy(results.at[rest], results.at[rest], b_send).wait()
    others = pl.ds(0, depth - 1)
    pltpu.make_async_copy(rows_two.at[others], rows_two.at[others], f_send.at[0]).wait()
    for n in range(slots - 1):
        pltpu.make_async_copy(rows.at[n, others], rows.at[n, others], f_send.at[n + 1]).wait()
    for j in range(slots):

        @pl.when(place < last)
        def _():
            to_next(j).wait_send()

        @pl.when(place > 0)
        def _():
            to_previous(j).wait_send()


def body(increment, trajectory, input_weight, bias, output_weight, correlation):
    slots, fields, rows, nx = increment.shape
    pick_wide, pick_narrow, pick_out = (jnp.asarray(x, BF16) for x in selections())
    depth = lax.axis_size("tm")
    time = correlation.shape[1]
    perm = np.zeros((time, time + depth), np.float32)
    for e in range(depth):
        for j in range(slots):
            perm[e * slots + j, j * depth + e] = 1.0
        if e + 1 < depth:
            perm[(e + 1) * slots, time + e] = 1.0
    tables = (
        jnp.transpose(input_weight, (2, 3, 1, 0)), bias[None, :], jnp.transpose(output_weight, (2, 3, 0, 1)),
        pick_wide, pick_narrow, pick_out, jnp.asarray(perm, BF16),
    )
    local = increment.shape
    halo = (slots, 2, 2 * PAIR, nx)
    hidden = (14 * CHANNELS, 2 * nx)
    message = (slots - 1, depth, nx // 128, 128)
    dma = pltpu.SemaphoreType.DMA
    return pl.pallas_call(
        cycle_kernel,
        out_shape=pltpu.VMEM(local, F32),
        in_specs=[HBM] * 10,
        out_specs=VMEM,
        scratch_shapes=[pltpu.VMEM(x.shape, x.dtype) for x in tables]
        + [
            pltpu.VMEM(local, F32),
            pltpu.VMEM(local, F32),
            pltpu.VMEM(halo, F32),
            pltpu.VMEM(halo, F32),
            pltpu.VMEM(halo, F32),
            pltpu.VMEM(halo, F32),
            pltpu.VMEM((128, 128), F32),
            pltpu.VMEM((4 * TAPS, 128), F32),
            pltpu.VMEM((4 * CHANNELS, 28 * PAIR), BF16),
            pltpu.VMEM((2 * CHANNELS, 20 * PAIR), BF16),
            pltpu.VMEM((2, 18 * PAIR, 256), BF16),
            pltpu.VMEM((2, 12 * PAIR, 256), BF16),
            pltpu.VMEM((2 * PAIR, 2 * nx), F32),
            pltpu.VMEM((4, 28 * PAIR, 2 * nx), BF16),
            pltpu.VMEM(hidden, BF16),
            pltpu.VMEM(hidden, BF16),
            pltpu.VMEM((depth, 2, nx // 128, 128), F32),
            pltpu.VMEM((depth, 2, nx // 128, 128), F32),
            pltpu.VMEM(message, F32),
            pltpu.VMEM(message, F32),
            pltpu.VMEM((time, nx // 128, 128), F32),
            pltpu.VMEM((time, nx), F32),
            pltpu.VMEM((time, nx // 128, 128), F32),
            pltpu.VMEM((time, time), F32),
            dma((2, slots)), dma((len(tables),)), dma, pltpu.SemaphoreType.REGULAR((2,)), dma((2, slots)), dma((2, slots)),
            dma((slots,)), dma((slots,)), dma, dma,
        ],
        compiler_params=pltpu.CompilerParams(collective_id=0, has_side_effects=True),
        name="cycle",
    )(increment, trajectory, *tables, correlation)


def solution(mesh):
    split_spec = P("tm", None, "space", None)
    return jax.shard_map(
        body,
        mesh=mesh,
        in_specs=(split_spec, split_spec, P(), P(), P(), P()),
        out_specs=split_spec,
        check_vma=False,
    )
```

```python
import functools

import jax
import jax.numpy as jnp
import numpy as np
from jax import lax
from jax.experimental import pallas as pl
from jax.experimental.pallas import tpu as pltpu
from jax.sharding import PartitionSpec as P

MESH = pl.DeviceIdType.MESH
F32, BF16 = jnp.float32, jnp.bfloat16
VMEM = pl.BlockSpec(memory_space=pltpu.VMEM)
HBM = pl.BlockSpec(memory_space=pl.ANY)

ROWS, FIELDS, CHANNELS = 8, 4, 32
PAIR = 2 * FIELDS
TAPS = 48
BIAS = 36
HALVES = ((-3, 3), (-1, 3))


def tap(a, b, f):
    return (a * 3 + b) * FIELDS + f


def selections():
    wide = np.zeros((4, 2 * TAPS, 28 * PAIR), np.float32)
    narrow = np.zeros((2, 2 * TAPS, 20 * PAIR), np.float32)
    for table, pairs in ((wide, 3), (narrow, 2)):
        third = pairs * 3 * PAIR
        for i in range(table.shape[0]):
            table[i, BIAS, 3 * third] = 1.0
            table[i, TAPS + BIAS, 3 * third + 1] = 1.0
            for k in range(pairs):
                for b in range(3):
                    for f in range(FIELDS):
                        for r in range(2):
                            a = 2 * k + r - i
                            if 0 <= a < 3:
                                line = (k * 3 + b) * PAIR + 2 * f + r
                                table[i, tap(a, b, f), line] = 1.0
                                table[i, tap(a, b, f), third + line] = 1.0
                                table[i, TAPS + tap(a, b, f), 2 * third + line] = 1.0
    out = np.zeros((2, 9 * PAIR, 4 * TAPS), np.float32)
    for k in range(3):
        for b in range(3):
            for f in range(FIELDS):
                for r in range(2):
                    for a in range(3):
                        i = 2 * k + r + a
                        out[i // 4, (k * 3 + b) * PAIR + 2 * f + r, i % 4 * TAPS + tap(a, b, f)] = 1.0
    return wide, narrow, out


def far_first(wide, deep):
    offsets = [(p, q) for p in range(wide) for q in range(deep) if p or q]
    hops = lambda n, size: min(n, size - n)
    return sorted(offsets, key=lambda o: (-hops(o[0], wide) - hops(o[1], deep), -hops(o[1], deep), o))


def split(x):
    high = x.astype(BF16)
    return high, (x - high.astype(F32)).astype(BF16)


def dot(a, b):
    return jnp.dot(a, b, preferred_element_type=F32)


def cycle_kernel(
    inc_hbm, traj_hbm, *refs,
):
    count = 7
    tables_hbm, corr, refs = refs[:count], refs[count], refs[count + 1 :]
    out, tables, refs = refs[0], refs[1 : count + 1], refs[count + 1 :]
    cycle(inc_hbm, traj_hbm, tables_hbm, corr, out, tables, *refs)


def cycle(
    inc_hbm, traj_hbm, tables_hbm, corr, out, tables,
    inc, traj, up, down, top, bot,
    taps_in, taps_out, t1, t1n, t2_first, t2_second,
    ones, xs, hh, hl, rows_two, cols_two, rows, cols, results, partial, back, cmat,
    in_sem, table_sem, c_sem, met, halo_send, halo_recv, f_send, f_recv, b_send, b_recv,
):
    slots, nx = inc.shape[0], inc.shape[3]
    quarter = nx // 128
    depth = lax.axis_size("tm")
    width = depth // FIELDS
    me = lax.axis_index("tm")
    my_field, my_row = lax.div(me, width), lax.rem(me, width)
    place = lax.axis_index("space")
    last = lax.axis_size("space") - 1
    order = range(slots)

    barrier = pltpu.get_barrier_semaphore()

    fields = [my_field] + [lax.rem(my_field + p, FIELDS) for p in range(1, FIELDS)]
    strips = [my_row] + [lax.rem(my_row + p, width) for p in range(1, width)]
    peers = [(fields[p], strips[q]) for p, q in far_first(FIELDS, width)]

    def device(peer):
        return {"tm": peer[0] * width + peer[1]}

    beside = [(my_field, strips[q]) for q in (2, -2)]
    close = [(my_field, strips[q]) for q in (1, -1)]
    across = [(fields[p], my_row) for p in range(1, FIELDS)]

    def say(sem, devices):
        for d in devices:
            pl.semaphore_signal(sem, inc=1, device_id=device(d), device_id_type=MESH)

    w_in, w_bias, w_out, pick_wide, pick_narrow, pick_out, perm = tables

    @pl.when(place > 0)
    def _():
        pl.semaphore_signal(barrier, inc=1, device_id={"space": place - 1}, device_id_type=MESH)

    @pl.when(place < last)
    def _():
        pl.semaphore_signal(barrier, inc=1, device_id={"space": place + 1}, device_id_type=MESH)

    def inputs(j):
        return (
            pltpu.make_async_copy(traj_hbm.at[j], traj.at[j], in_sem.at[0, j]),
            pltpu.make_async_copy(inc_hbm.at[j], inc.at[j], in_sem.at[1, j]),
        )

    say(barrier, beside + across + close)
    for j in order:
        for copy in inputs(j):
            copy.start()

    table_copies = [pltpu.make_async_copy(*x, table_sem.at[n]) for n, x in enumerate(zip(tables_hbm, tables))]
    for copy in table_copies:
        copy.start()
    c_copy = pltpu.make_async_copy(corr.at[my_field], cmat, c_sem)
    c_copy.start()

    def pack(j):
        for array, source in enumerate((traj, inc)):
            for f in range(FIELDS):
                for half, target in enumerate((up, down)):
                    for k in range(2):
                        r = 4 * half + 2 * k
                        target[j, array, PAIR * k + 2 * f : PAIR * k + 2 * f + 2, :] = source[j, f, r : r + 2, :]

    def to_next(j):
        return pltpu.make_async_remote_copy(
            down.at[j], top.at[j], halo_send.at[0, j], halo_recv.at[0, j],
            device_id={"space": place + 1}, device_id_type=MESH,
        )

    def to_previous(j):
        return pltpu.make_async_remote_copy(
            up.at[j], bot.at[j], halo_send.at[1, j], halo_recv.at[1, j],
            device_id={"space": place - 1}, device_id_type=MESH,
        )

    for n, j in enumerate(order):
        for copy in inputs(j):
            copy.wait()
        pack(j)
        if n == 0:
            pl.semaphore_wait(barrier, len(beside + across + close) + jnp.minimum(place, 1) + jnp.minimum(last - place, 1))
            say(met.at[0], beside)

        @pl.when(place < last)
        def _():
            to_next(j).start()

        @pl.when(place > 0)
        def _():
            to_previous(j).start()

    for copy in table_copies:
        copy.wait()

    taps_in[...] = jnp.zeros_like(taps_in)
    taps_out[...] = jnp.zeros_like(taps_out)
    for a in range(3):
        for b in range(3):
            at = tap(a, b, 0)
            taps_in[at : at + FIELDS, :CHANNELS] = w_in[a, b]
            w = 0.5 * w_out[a, b]
            for q in range(4):
                taps_out[q * TAPS + at : q * TAPS + at + FIELDS, q * CHANNELS : q * CHANNELS + CHANNELS] = w
    taps_in[BIAS : BIAS + 1, :CHANNELS] = w_bias[...]
    w = taps_in[:TAPS, :]
    high = w.astype(BF16).astype(F32)
    taps_in[:TAPS, :] = high
    taps_in[TAPS : 2 * TAPS, :] = w - high
    w = jnp.transpose(taps_in[...])[:CHANNELS]
    w = w[:, : 2 * TAPS].astype(BF16)
    for i in range(4):
        t1[CHANNELS * i : CHANNELS * i + CHANNELS, :] = dot(w, pick_wide[i]).astype(BF16)
    for i in range(2):
        t1n[CHANNELS * i : CHANNELS * i + CHANNELS, :] = dot(w, pick_narrow[i]).astype(BF16)
    lane_row = lax.shift_right_logical(lax.broadcasted_iota(jnp.int32, (1, 128), 1), 5) + place * ROWS
    for n, part in enumerate(split(taps_out[...])):
        for g in range(2):
            x = dot(pick_out[g], part)
            for step_id, target in enumerate((t2_first, t2_second)):
                lines = target.shape[1] // 2
                for half in range(2):
                    row = lane_row + (HALVES[step_id][half] + 4 * g)
                    keep = jnp.where((row >= 0) & (row < (last + 1) * ROWS), x[:lines], 0.0)
                    target[half, n * lines : n * lines + lines, 128 * g : 128 * g + 128] = keep.astype(BF16)

    @pl.when(place == 0)
    def _():
        top[...] = jnp.zeros_like(top)

    @pl.when(place == last)
    def _():
        bot[...] = jnp.zeros_like(bot)

    pl.semaphore_wait(met.at[0], len(beside))
    say(met.at[1], across)

    column = lax.broadcasted_iota(jnp.int32, (1, 128), 1)
    first, final = column == 0, column == 127

    def from_left(x):
        y = pltpu.roll(x, 1, 1)
        return jnp.concatenate([jnp.where(first, 0.0, y[:, :128]), y[:, 128:]], axis=1)

    def from_right(x):
        y = pltpu.roll(x, nx - 1, 1)
        return jnp.concatenate([y[:, : nx - 128], jnp.where(final, 0.0, y[:, nx - 128 :])], axis=1)

    ones[...] = jnp.where(
        (lax.broadcasted_iota(jnp.int32, ones.shape, 0) < 2)
        & (lax.broadcasted_iota(jnp.int32, ones.shape, 1) < nx),
        1.0,
        0.0,
    )

    def step(state, step_id):
        pairs = len(state[0])
        outs = pairs - 2
        mids = 2 * outs + 2
        highs, lows = [], []
        for k in range(pairs):
            high, low = [], []
            for array in range(2):
                x = state[array][k]
                x = jnp.concatenate([from_left(x), x, from_right(x)], axis=0)
                h = x.astype(BF16).astype(F32)
                high.append(h)
                low.append(x - h)
            highs.append(jnp.concatenate(high, axis=1))
            lows.append(jnp.concatenate(low, axis=1))
        spans = [(g, 3) for g in range(0, pairs - 2, 2)] + [(pairs - 2, 2)]
        for g, n in spans:
            high = highs[g : g + n]
            pad = [ones[:PAIR]] if n == 3 else [ones[...]]
            value = jnp.concatenate(high + lows[g : g + n] + high + pad, axis=0).astype(BF16)
            xs[g // 2, : value.shape[0], :] = value
        for n in range(0, nx, 256):
            s, t = slice(n, n + 256), slice(nx + n, nx + n + 256)
            at = 0
            for g, count in spans:
                table, many = (t1, 4) if count == 3 else (t1n, 2)
                depth_in = table.shape[1]
                zs = dot(table[...], xs[g // 2, :depth_in, s])
                zt = dot(table[...], xs[g // 2, :depth_in, t])
                h = jnp.tanh(zs)
                slope = (1.0 - h * h) * zt
                lines = slice(at, at + many * CHANNELS)
                hh[lines, s], hl[lines, s] = split(h)
                hh[lines, t], hl[lines, t] = split(slope)
                at += many * CHANNELS
        new = [[], []]
        wide, deep = outs // 2, (outs + 2) * CHANNELS
        table = (t2_first, t2_second)[step_id]
        for array in range(2):
            lane = slice(array * nx, array * nx + nx)
            for half in range(2):
                start = half * outs * CHANNELS
                lines = 3 * PAIR * wide
                both = dot(table[half, :, :deep], hh[start : start + deep, lane])
                taps = both[:lines] + both[lines:] + dot(table[half, :lines, :deep], hl[start : start + deep, lane])
                for k in range(wide):
                    left, middle, right = (taps[PAIR * n : PAIR * n + PAIR] for n in range(3 * k, 3 * k + 3))
                    new[array].append(state[array][half * wide + k + 1] + (from_left(left) + middle + from_right(right)))
        return new

    def line_of(peer):
        f, r = peer
        return lax.div(r, 2) * PAIR + 2 * f + lax.rem(r, 2)

    def send_lines(phase, outgoing, incoming):
        for peer in peers:
            pltpu.make_async_remote_copy(
                outgoing.at[line_of(peer)], incoming.at[me], f_send.at[phase], f_recv.at[phase],
                device_id=device(peer), device_id_type=MESH,
            ).start()
        own = outgoing.at[line_of((my_field, my_row))]
        pltpu.make_async_copy(own, incoming.at[me], f_recv.at[phase]).start()

    def increment_lines(j):
        return jnp.concatenate([up[j, 1], down[j, 1]], axis=0)

    @pl.loop(0, slots)
    def _(i):
        slot = i

        @pl.when(place > 0)
        def _():
            to_next(slot).wait_recv()

        @pl.when(place < last)
        def _():
            to_previous(slot).wait_recv()

        state = []
        for array in range(2):
            parts = [x[slot, array] for x in (top, up, down, bot)]
            state.append([x[PAIR * k : PAIR * k + PAIR] for x in parts for k in range(2)])
        state = step(state, 0)
        for array in range(2):
            state[array][0] = jnp.where(place > 0, state[array][0], 0.0)
            state[array][-1] = jnp.where(place < last, state[array][-1], 0.0)

        state = step(state, 1)
        forecast = jnp.concatenate(state[1], axis=0)

        @pl.when(i == 0)
        def _():
            pair = (increment_lines(0), increment_lines(1) - forecast)
            lines = rows_two.reshape(depth * 2 * quarter, 128)
            for n, value in enumerate(pair):
                for q in range(quarter):
                    lines[pl.ds(n * quarter + q, depth, stride=2 * quarter), :] = value[:, 128 * q : 128 * q + 128]
            pl.semaphore_wait(met.at[1], len(across))
            send_lines(0, rows_two, cols_two)

        @pl.when(i > 0)
        def _():
            following = increment_lines(jnp.minimum(i + 1, slots - 1))
            value = jnp.where(i < slots - 1, following, 0.0) - forecast
            lines = rows.reshape((slots - 1) * depth * quarter, 128)
            for q in range(quarter):
                lines[pl.ds((i - 1) * depth * quarter + q, depth, stride=quarter), :] = value[:, 128 * q : 128 * q + 128]
            send_lines(i, rows.at[i - 1], cols.at[i - 1])

    c_copy.wait()
    ch, cl = split(cmat[...])
    both = jnp.concatenate([ch, cl], axis=0)
    both = dot(both, perm[...]).astype(BF16)
    time = slots * depth
    two = cols_two.reshape(depth * 2 * quarter, 128)
    one = cols.reshape((slots - 1) * depth * quarter, 128)
    sums = results.reshape(time * quarter, 128)

    def received(x, start, stride):
        return jnp.concatenate([x[pl.ds(start + q, depth, stride=stride), :] for q in range(quarter)], axis=1)

    def product(columns, values):
        vh, vl = split(values)
        x = dot(both[:, columns], vh)
        return x[:time] + x[time:] + dot(both[:time, columns], vl)

    pltpu.make_async_copy(cols_two, cols_two, f_recv.at[0]).wait()
    values = [received(two, 0, 2 * quarter), received(two, quarter, 2 * quarter)]
    for n in range(slots - 2):
        pltpu.make_async_copy(cols.at[n], cols.at[n], f_recv.at[n + 1]).wait()
        values.append(received(one, n * depth * quarter, quarter))
    partial[...] = product(slice(0, time), jnp.concatenate(values, axis=0))
    pltpu.make_async_copy(cols.at[slots - 2], cols.at[slots - 2], f_recv.at[slots - 1]).wait()
    total = partial[...] + product(slice(time, time + depth), received(one, (slots - 2) * depth * quarter, quarter))
    for q in range(quarter):
        sums[pl.ds(q, time, stride=quarter), :] = total[:, 128 * q : 128 * q + 128]
    mine = pl.ds(me * slots, slots)
    for peer in peers:
        pltpu.make_async_remote_copy(
            results.at[pl.ds((peer[0] * width + peer[1]) * slots, slots)], back.at[mine], b_send, b_recv.at[my_field],
            device_id=device(peer), device_id_type=MESH,
        ).start()
    pltpu.make_async_copy(results.at[mine], back.at[mine], b_recv.at[my_field]).start()

    lines = back.reshape(depth * slots * quarter, 128)
    for f in range(FIELDS):
        group = back.at[pl.ds(f * width * slots, width * slots)]
        pltpu.make_async_copy(group, group, b_recv.at[f]).wait()
        for j in range(slots):
            for q in range(quarter):
                out[j, f, :, 128 * q : 128 * q + 128] = lines[
                    pl.ds((f * width * slots + j) * quarter + q, ROWS, stride=slots * quarter), :
                ]
    rest = pl.ds(0, (depth - 1) * slots)
    pltpu.make_async_copy(results.at[rest], results.at[rest], b_send).wait()
    others = pl.ds(0, depth - 1)
    pltpu.make_async_copy(rows_two.at[others], rows_two.at[others], f_send.at[0]).wait()
    for n in range(slots - 1):
        pltpu.make_async_copy(rows.at[n, others], rows.at[n, others], f_send.at[n + 1]).wait()
    for j in range(slots):

        @pl.when(place < last)
        def _():
            to_next(j).wait_send()

        @pl.when(place > 0)
        def _():
            to_previous(j).wait_send()


def body(increment, trajectory, input_weight, bias, output_weight, correlation):
    slots, fields, rows, nx = increment.shape
    pick_wide, pick_narrow, pick_out = (jnp.asarray(x, BF16) for x in selections())
    depth = lax.axis_size("tm")
    time = correlation.shape[1]
    perm = np.zeros((time, time + depth), np.float32)
    for e in range(depth):
        for j in range(slots):
            perm[e * slots + j, j * depth + e] = 1.0
        if e + 1 < depth:
            perm[(e + 1) * slots, time + e] = 1.0
    tables = (
        jnp.transpose(input_weight, (2, 3, 1, 0)), bias[None, :], jnp.transpose(output_weight, (2, 3, 0, 1)),
        pick_wide, pick_narrow, pick_out, jnp.asarray(perm, BF16),
    )
    local = increment.shape
    halo = (slots, 2, 2 * PAIR, nx)
    hidden = (14 * CHANNELS, 2 * nx)
    message = (slots - 1, depth, nx // 128, 128)
    dma = pltpu.SemaphoreType.DMA
    return pl.pallas_call(
        cycle_kernel,
        out_shape=pltpu.VMEM(local, F32),
        in_specs=[HBM] * 10,
        out_specs=VMEM,
        scratch_shapes=[pltpu.VMEM(x.shape, x.dtype) for x in tables]
        + [
            pltpu.VMEM(local, F32),
            pltpu.VMEM(local, F32),
            pltpu.VMEM(halo, F32),
            pltpu.VMEM(halo, F32),
            pltpu.VMEM(halo, F32),
            pltpu.VMEM(halo, F32),
            pltpu.VMEM((128, 128), F32),
            pltpu.VMEM((4 * TAPS, 128), F32),
            pltpu.VMEM((4 * CHANNELS, 28 * PAIR), BF16),
            pltpu.VMEM((2 * CHANNELS, 20 * PAIR), BF16),
            pltpu.VMEM((2, 18 * PAIR, 256), BF16),
            pltpu.VMEM((2, 12 * PAIR, 256), BF16),
            pltpu.VMEM((2 * PAIR, 2 * nx), F32),
            pltpu.VMEM((4, 28 * PAIR, 2 * nx), BF16),
            pltpu.VMEM(hidden, BF16),
            pltpu.VMEM(hidden, BF16),
            pltpu.VMEM((depth, 2, nx // 128, 128), F32),
            pltpu.VMEM((depth, 2, nx // 128, 128), F32),
            pltpu.VMEM(message, F32),
            pltpu.VMEM(message, F32),
            pltpu.VMEM((time, nx // 128, 128), F32),
            pltpu.VMEM((time, nx), F32),
            pltpu.VMEM((time, nx // 128, 128), F32),
            pltpu.VMEM((time, time), F32),
            dma((2, slots)), dma((len(tables),)), dma, pltpu.SemaphoreType.REGULAR((2,)), dma((2, slots)), dma((2, slots)),
            dma((slots,)), dma((slots,)), dma, dma((FIELDS,)),
        ],
        compiler_params=pltpu.CompilerParams(collective_id=0, has_side_effects=True),
        name="cycle",
    )(increment, trajectory, *tables, correlation)


def solution(mesh):
    split_spec = P("tm", None, "space", None)
    return jax.shard_map(
        body,
        mesh=mesh,
        in_specs=(split_spec, split_spec, P(), P(), P(), P()),
        out_specs=split_spec,
        check_vma=False,
    )
```

```python
import functools

import jax
import jax.numpy as jnp
import numpy as np
from jax import lax
from jax.experimental import pallas as pl
from jax.experimental.pallas import tpu as pltpu
from jax.sharding import PartitionSpec as P

MESH = pl.DeviceIdType.MESH
F32, BF16 = jnp.float32, jnp.bfloat16
VMEM = pl.BlockSpec(memory_space=pltpu.VMEM)
HBM = pl.BlockSpec(memory_space=pl.ANY)

ROWS, FIELDS, CHANNELS = 8, 4, 32
PAIR = 2 * FIELDS
TAPS = 48
BIAS = 36
HALVES = ((-3, 3), (-1, 3))


def tap(a, b, f):
    return (a * 3 + b) * FIELDS + f


def selections():
    wide = np.zeros((4, 2 * TAPS, 28 * PAIR), np.float32)
    narrow = np.zeros((2, 2 * TAPS, 20 * PAIR), np.float32)
    for table, pairs in ((wide, 3), (narrow, 2)):
        third = pairs * 3 * PAIR
        for i in range(table.shape[0]):
            table[i, BIAS, 3 * third] = 1.0
            table[i, TAPS + BIAS, 3 * third + 1] = 1.0
            for k in range(pairs):
                for b in range(3):
                    for f in range(FIELDS):
                        for r in range(2):
                            a = 2 * k + r - i
                            if 0 <= a < 3:
                                line = (k * 3 + b) * PAIR + 2 * f + r
                                table[i, tap(a, b, f), line] = 1.0
                                table[i, tap(a, b, f), third + line] = 1.0
                                table[i, TAPS + tap(a, b, f), 2 * third + line] = 1.0
    out = np.zeros((2, 9 * PAIR, 4 * TAPS), np.float32)
    for k in range(3):
        for b in range(3):
            for f in range(FIELDS):
                for r in range(2):
                    for a in range(3):
                        i = 2 * k + r + a
                        out[i // 4, (k * 3 + b) * PAIR + 2 * f + r, i % 4 * TAPS + tap(a, b, f)] = 1.0
    return wide, narrow, out


def far_first(wide, deep):
    offsets = [(p, q) for p in range(wide) for q in range(deep) if p or q]
    hops = lambda n, size: min(n, size - n)
    return sorted(offsets, key=lambda o: (-hops(o[0], wide) - hops(o[1], deep), -hops(o[1], deep), o))


def split(x):
    high = x.astype(BF16)
    return high, (x - high.astype(F32)).astype(BF16)


def dot(a, b):
    return jnp.dot(a, b, preferred_element_type=F32)


def cycle_kernel(
    inc_hbm, traj_hbm, *refs,
):
    count = 7
    tables_hbm, corr, refs = refs[:count], refs[count], refs[count + 1 :]
    out, tables, refs = refs[0], refs[1 : count + 1], refs[count + 1 :]
    cycle(inc_hbm, traj_hbm, tables_hbm, corr, out, tables, *refs)


def cycle(
    inc_hbm, traj_hbm, tables_hbm, corr, out, tables,
    inc, traj, up, down, top, bot,
    taps_in, taps_out, t1, t1n, t2_first, t2_second,
    ones, xs, hh, hl, rows_two, cols_two, rows, cols, results, partial, back, cmat,
    in_sem, table_sem, c_sem, met, halo_send, halo_recv, f_send, f_recv, b_send, b_recv,
):
    slots, nx = inc.shape[0], inc.shape[3]
    quarter = nx // 128
    depth = lax.axis_size("tm")
    width = depth // FIELDS
    me = lax.axis_index("tm")
    my_field, my_row = lax.div(me, width), lax.rem(me, width)
    place = lax.axis_index("space")
    last = lax.axis_size("space") - 1
    order = range(slots)

    barrier = pltpu.get_barrier_semaphore()

    fields = [my_field] + [lax.rem(my_field + p, FIELDS) for p in range(1, FIELDS)]
    strips = [my_row] + [lax.rem(my_row + p, width) for p in range(1, width)]
    peers = [(fields[p], strips[q]) for p, q in far_first(FIELDS, width)]

    def device(peer):
        return {"tm": peer[0] * width + peer[1]}

    beside = [(my_field, strips[q]) for q in (2, -2)]
    close = [(my_field, strips[q]) for q in (1, -1)]
    across = [(fields[p], my_row) for p in range(1, FIELDS)]

    def say(sem, devices):
        for d in devices:
            pl.semaphore_signal(sem, inc=1, device_id=device(d), device_id_type=MESH)

    w_in, w_bias, w_out, pick_wide, pick_narrow, pick_out, perm = tables

    @pl.when(place > 0)
    def _():
        pl.semaphore_signal(barrier, inc=1, device_id={"space": place - 1}, device_id_type=MESH)

    @pl.when(place < last)
    def _():
        pl.semaphore_signal(barrier, inc=1, device_id={"space": place + 1}, device_id_type=MESH)

    def inputs(j):
        return (
            pltpu.make_async_copy(traj_hbm.at[j], traj.at[j], in_sem.at[0, j]),
            pltpu.make_async_copy(inc_hbm.at[j], inc.at[j], in_sem.at[1, j]),
        )

    say(barrier, beside + across + close)
    for j in order:
        for copy in inputs(j):
            copy.start()

    table_copies = [pltpu.make_async_copy(*x, table_sem.at[n]) for n, x in enumerate(zip(tables_hbm, tables))]
    for copy in table_copies:
        copy.start()
    c_copy = pltpu.make_async_copy(corr.at[my_field], cmat, c_sem)
    c_copy.start()

    def pack(j):
        for array, source in enumerate((traj, inc)):
            for f in range(FIELDS):
                for half, target in enumerate((up, down)):
                    for k in range(2):
                        r = 4 * half + 2 * k
                        target[j, array, PAIR * k + 2 * f : PAIR * k + 2 * f + 2, :] = source[j, f, r : r + 2, :]

    def to_next(j):
        return pltpu.make_async_remote_copy(
            down.at[j], top.at[j], halo_send.at[0, j], halo_recv.at[0, j],
            device_id={"space": place + 1}, device_id_type=MESH,
        )

    def to_previous(j):
        return pltpu.make_async_remote_copy(
            up.at[j], bot.at[j], halo_send.at[1, j], halo_recv.at[1, j],
            device_id={"space": place - 1}, device_id_type=MESH,
        )

    for n, j in enumerate(order):
        for copy in inputs(j):
            copy.wait()
        pack(j)
        if n == 0:
            pl.semaphore_wait(barrier, len(beside + across + close) + jnp.minimum(place, 1) + jnp.minimum(last - place, 1))
            say(met.at[0], beside)

        @pl.when(place < last)
        def _():
            to_next(j).start()

        @pl.when(place > 0)
        def _():
            to_previous(j).start()

    for copy in table_copies:
        copy.wait()

    taps_in[...] = jnp.zeros_like(taps_in)
    taps_out[...] = jnp.zeros_like(taps_out)
    for a in range(3):
        for b in range(3):
            at = tap(a, b, 0)
            taps_in[at : at + FIELDS, :CHANNELS] = w_in[a, b]
            w = 0.5 * w_out[a, b]
            for q in range(4):
                taps_out[q * TAPS + at : q * TAPS + at + FIELDS, q * CHANNELS : q * CHANNELS + CHANNELS] = w
    taps_in[BIAS : BIAS + 1, :CHANNELS] = w_bias[...]
    w = taps_in[:TAPS, :]
    high = w.astype(BF16).astype(F32)
    taps_in[:TAPS, :] = high
    taps_in[TAPS : 2 * TAPS, :] = w - high
    w = jnp.transpose(taps_in[...])[:CHANNELS]
    w = w[:, : 2 * TAPS].astype(BF16)
    for i in range(4):
        t1[CHANNELS * i : CHANNELS * i + CHANNELS, :] = dot(w, pick_wide[i]).astype(BF16)
    for i in range(2):
        t1n[CHANNELS * i : CHANNELS * i + CHANNELS, :] = dot(w, pick_narrow[i]).astype(BF16)
    lane_row = lax.shift_right_logical(lax.broadcasted_iota(jnp.int32, (1, 128), 1), 5) + place * ROWS
    for n, part in enumerate(split(taps_out[...])):
        for g in range(2):
            x = dot(pick_out[g], part)
            for step_id, target in enumerate((t2_first, t2_second)):
                lines = target.shape[1] // 2
                for half in range(2):
                    row = lane_row + (HALVES[step_id][half] + 4 * g)
                    keep = jnp.where((row >= 0) & (row < (last + 1) * ROWS), x[:lines], 0.0)
                    target[half, n * lines : n * lines + lines, 128 * g : 128 * g + 128] = keep.astype(BF16)

    @pl.when(place == 0)
    def _():
        top[...] = jnp.zeros_like(top)

    @pl.when(place == last)
    def _():
        bot[...] = jnp.zeros_like(bot)

    pl.semaphore_wait(met.at[0], len(beside))
    say(met.at[1], across)

    column = lax.broadcasted_iota(jnp.int32, (1, 128), 1)
    first, final = column == 0, column == 127

    def from_left(x):
        y = pltpu.roll(x, 1, 1)
        return jnp.concatenate([jnp.where(first, 0.0, y[:, :128]), y[:, 128:]], axis=1)

    def from_right(x):
        y = pltpu.roll(x, nx - 1, 1)
        return jnp.concatenate([y[:, : nx - 128], jnp.where(final, 0.0, y[:, nx - 128 :])], axis=1)

    ones[...] = jnp.where(
        (lax.broadcasted_iota(jnp.int32, ones.shape, 0) < 2)
        & (lax.broadcasted_iota(jnp.int32, ones.shape, 1) < nx),
        1.0,
        0.0,
    )

    def step(state, step_id):
        pairs = len(state[0])
        outs = pairs - 2
        mids = 2 * outs + 2
        highs, lows = [], []
        for k in range(pairs):
            high, low = [], []
            for array in range(2):
                x = state[array][k]
                x = jnp.concatenate([from_left(x), x, from_right(x)], axis=0)
                h = x.astype(BF16).astype(F32)
                high.append(h)
                low.append(x - h)
            highs.append(jnp.concatenate(high, axis=1))
            lows.append(jnp.concatenate(low, axis=1))
        spans = [(g, 3) for g in range(0, pairs - 2, 2)] + [(pairs - 2, 2)]
        for g, n in spans:
            high = highs[g : g + n]
            pad = [ones[:PAIR]] if n == 3 else [ones[...]]
            value = jnp.concatenate(high + lows[g : g + n] + high + pad, axis=0).astype(BF16)
            xs[g // 2, : value.shape[0], :] = value
        for n in range(0, nx, 256):
            s, t = slice(n, n + 256), slice(nx + n, nx + n + 256)
            at = 0
            made = []
            for g, count in spans:
                table, many = (t1, 4) if count == 3 else (t1n, 2)
                depth_in = table.shape[1]
                made.append([dot(table[...], xs[g // 2, :depth_in, x]) for x in (s, t)])
            for zs, zt in made:
                h = jnp.tanh(zs)
                slope = (1.0 - h * h) * zt
                lines = slice(at, at + zs.shape[0])
                hh[lines, s], hl[lines, s] = split(h)
                hh[lines, t], hl[lines, t] = split(slope)
                at += zs.shape[0]
        new = [[], []]
        wide, deep = outs // 2, (outs + 2) * CHANNELS
        table = (t2_first, t2_second)[step_id]
        for array in range(2):
            lane = slice(array * nx, array * nx + nx)
            for half in range(2):
                start = half * outs * CHANNELS
                lines = 3 * PAIR * wide
                both = dot(table[half, :, :deep], hh[start : start + deep, lane])
                taps = both[:lines] + both[lines:] + dot(table[half, :lines, :deep], hl[start : start + deep, lane])
                for k in range(wide):
                    left, middle, right = (taps[PAIR * n : PAIR * n + PAIR] for n in range(3 * k, 3 * k + 3))
                    new[array].append(state[array][half * wide + k + 1] + (from_left(left) + middle + from_right(right)))
        return new

    def line_of(peer):
        f, r = peer
        return lax.div(r, 2) * PAIR + 2 * f + lax.rem(r, 2)

    def send_lines(phase, outgoing, incoming):
        for peer in peers:
            pltpu.make_async_remote_copy(
                outgoing.at[line_of(peer)], incoming.at[me], f_send.at[phase], f_recv.at[phase],
                device_id=device(peer), device_id_type=MESH,
            ).start()
        own = outgoing.at[line_of((my_field, my_row))]
        pltpu.make_async_copy(own, incoming.at[me], f_recv.at[phase]).start()

    def increment_lines(j):
        return jnp.concatenate([up[j, 1], down[j, 1]], axis=0)

    @pl.loop(0, slots)
    def _(i):
        slot = i

        @pl.when(place > 0)
        def _():
            to_next(slot).wait_recv()

        @pl.when(place < last)
        def _():
            to_previous(slot).wait_recv()

        state = []
        for array in range(2):
            parts = [x[slot, array] for x in (top, up, down, bot)]
            state.append([x[PAIR * k : PAIR * k + PAIR] for x in parts for k in range(2)])
        state = step(state, 0)
        for array in range(2):
            state[array][0] = jnp.where(place > 0, state[array][0], 0.0)
            state[array][-1] = jnp.where(place < last, state[array][-1], 0.0)

        state = step(state, 1)
        forecast = jnp.concatenate(state[1], axis=0)

        @pl.when(i == 0)
        def _():
            pair = (increment_lines(0), increment_lines(1) - forecast)
            lines = rows_two.reshape(depth * 2 * quarter, 128)
            for n, value in enumerate(pair):
                for q in range(quarter):
                    lines[pl.ds(n * quarter + q, depth, stride=2 * quarter), :] = value[:, 128 * q : 128 * q + 128]
            pl.semaphore_wait(met.at[1], len(across))
            send_lines(0, rows_two, cols_two)

        @pl.when(i > 0)
        def _():
            following = increment_lines(jnp.minimum(i + 1, slots - 1))
            value = jnp.where(i < slots - 1, following, 0.0) - forecast
            lines = rows.reshape((slots - 1) * depth * quarter, 128)
            for q in range(quarter):
                lines[pl.ds((i - 1) * depth * quarter + q, depth, stride=quarter), :] = value[:, 128 * q : 128 * q + 128]
            send_lines(i, rows.at[i - 1], cols.at[i - 1])

    c_copy.wait()
    ch, cl = split(cmat[...])
    both = jnp.concatenate([ch, cl], axis=0)
    both = dot(both, perm[...]).astype(BF16)
    time = slots * depth
    two = cols_two.reshape(depth * 2 * quarter, 128)
    one = cols.reshape((slots - 1) * depth * quarter, 128)
    sums = results.reshape(time * quarter, 128)

    def received(x, start, stride):
        return jnp.concatenate([x[pl.ds(start + q, depth, stride=stride), :] for q in range(quarter)], axis=1)

    def product(columns, values):
        vh, vl = split(values)
        x = dot(both[:, columns], vh)
        return x[:time] + x[time:] + dot(both[:time, columns], vl)

    pltpu.make_async_copy(cols_two, cols_two, f_recv.at[0]).wait()
    values = [received(two, 0, 2 * quarter), received(two, quarter, 2 * quarter)]
    for n in range(slots - 2):
        pltpu.make_async_copy(cols.at[n], cols.at[n], f_recv.at[n + 1]).wait()
        values.append(received(one, n * depth * quarter, quarter))
    partial[...] = product(slice(0, time), jnp.concatenate(values, axis=0))
    pltpu.make_async_copy(cols.at[slots - 2], cols.at[slots - 2], f_recv.at[slots - 1]).wait()
    total = partial[...] + product(slice(time, time + depth), received(one, (slots - 2) * depth * quarter, quarter))
    for q in range(quarter):
        sums[pl.ds(q, time, stride=quarter), :] = total[:, 128 * q : 128 * q + 128]
    mine = pl.ds(me * slots, slots)
    for peer in peers:
        pltpu.make_async_remote_copy(
            results.at[pl.ds((peer[0] * width + peer[1]) * slots, slots)], back.at[mine], b_send, b_recv,
            device_id=device(peer), device_id_type=MESH,
        ).start()
    pltpu.make_async_copy(results.at[mine], back.at[mine], b_recv).start()

    pltpu.make_async_copy(back, back, b_recv).wait()
    lines = back.reshape(depth * slots * quarter, 128)
    for j in range(slots):
        for f in range(FIELDS):
            for q in range(quarter):
                out[j, f, :, 128 * q : 128 * q + 128] = lines[
                    pl.ds((f * width * slots + j) * quarter + q, ROWS, stride=slots * quarter), :
                ]
    rest = pl.ds(0, (depth - 1) * slots)
    pltpu.make_async_copy(results.at[rest], results.at[rest], b_send).wait()
    others = pl.ds(0, depth - 1)
    pltpu.make_async_copy(rows_two.at[others], rows_two.at[others], f_send.at[0]).wait()
    for n in range(slots - 1):
        pltpu.make_async_copy(rows.at[n, others], rows.at[n, others], f_send.at[n + 1]).wait()
    for j in range(slots):

        @pl.when(place < last)
        def _():
            to_next(j).wait_send()

        @pl.when(place > 0)
        def _():
            to_previous(j).wait_send()


def body(increment, trajectory, input_weight, bias, output_weight, correlation):
    slots, fields, rows, nx = increment.shape
    pick_wide, pick_narrow, pick_out = (jnp.asarray(x, BF16) for x in selections())
    depth = lax.axis_size("tm")
    time = correlation.shape[1]
    perm = np.zeros((time, time + depth), np.float32)
    for e in range(depth):
        for j in range(slots):
            perm[e * slots + j, j * depth + e] = 1.0
        if e + 1 < depth:
            perm[(e + 1) * slots, time + e] = 1.0
    tables = (
        jnp.transpose(input_weight, (2, 3, 1, 0)), bias[None, :], jnp.transpose(output_weight, (2, 3, 0, 1)),
        pick_wide, pick_narrow, pick_out, jnp.asarray(perm, BF16),
    )
    local = increment.shape
    halo = (slots, 2, 2 * PAIR, nx)
    hidden = (14 * CHANNELS, 2 * nx)
    message = (slots - 1, depth, nx // 128, 128)
    dma = pltpu.SemaphoreType.DMA
    return pl.pallas_call(
        cycle_kernel,
        out_shape=pltpu.VMEM(local, F32),
        in_specs=[HBM] * 10,
        out_specs=VMEM,
        scratch_shapes=[pltpu.VMEM(x.shape, x.dtype) for x in tables]
        + [
            pltpu.VMEM(local, F32),
            pltpu.VMEM(local, F32),
            pltpu.VMEM(halo, F32),
            pltpu.VMEM(halo, F32),
            pltpu.VMEM(halo, F32),
            pltpu.VMEM(halo, F32),
            pltpu.VMEM((128, 128), F32),
            pltpu.VMEM((4 * TAPS, 128), F32),
            pltpu.VMEM((4 * CHANNELS, 28 * PAIR), BF16),
            pltpu.VMEM((2 * CHANNELS, 20 * PAIR), BF16),
            pltpu.VMEM((2, 18 * PAIR, 256), BF16),
            pltpu.VMEM((2, 12 * PAIR, 256), BF16),
            pltpu.VMEM((2 * PAIR, 2 * nx), F32),
            pltpu.VMEM((4, 28 * PAIR, 2 * nx), BF16),
            pltpu.VMEM(hidden, BF16),
            pltpu.VMEM(hidden, BF16),
            pltpu.VMEM((depth, 2, nx // 128, 128), F32),
            pltpu.VMEM((depth, 2, nx // 128, 128), F32),
            pltpu.VMEM(message, F32),
            pltpu.VMEM(message, F32),
            pltpu.VMEM((time, nx // 128, 128), F32),
            pltpu.VMEM((time, nx), F32),
            pltpu.VMEM((time, nx // 128, 128), F32),
            pltpu.VMEM((time, time), F32),
            dma((2, slots)), dma((len(tables),)), dma, pltpu.SemaphoreType.REGULAR((2,)), dma((2, slots)), dma((2, slots)),
            dma((slots,)), dma((slots,)), dma, dma,
        ],
        compiler_params=pltpu.CompilerParams(collective_id=0, has_side_effects=True),
        name="cycle",
    )(increment, trajectory, *tables, correlation)


def solution(mesh):
    split_spec = P("tm", None, "space", None)
    return jax.shard_map(
        body,
        mesh=mesh,
        in_specs=(split_spec, split_spec, P(), P(), P(), P()),
        out_specs=split_spec,
        check_vma=False,
    )
```
